768 devices in a mesh: lon: 24 (over y_hi, z), lat: 32 (over x, y_lo, core).
Axes of the slice: x: 4, y: 8 (y_hi: 2, y_lo: 4; y = y_hi * 4 + y_lo), z: 12, core: 2. Of those that a mesh axis runs over, the one named last changes fastest.
Arguments:
- increment: float32 [4, 32, 256, 3072], P(None, None, 'lat', 'lon'), may hold values from -6 to 6
- coef_lon: float32 [4, 256, 3072], P(None, 'lat', 'lon'), may hold values from 0.4 to 0.49
- coef_lat: float32 [4, 256, 3072], P(None, 'lat', 'lon'), may hold values from 0.4 to 0.49
- obs_values: float32 [393216, 128], P(('lon', 'lat')), may hold values from -1.8 to 1.8
- obs_weight: float32 [393216, 128], P(('lon', 'lat')), may hold values from 0.25 to 4
- obs_operator: float32 [3, 128, 128], replicated, may hold values from -0.5 to 0.5
- obs_columns: int32 [393216], P(('lon', 'lat')), may hold values from 0 to 1023
- obs_types: int32 [393216], P(('lon', 'lat')), may hold values from 0 to 2
- obs_counts: int32 [24576], P(('lon', 'lat')), may hold values from 0 to 16, as said below
Outputs:
- gradient: float32 [4, 32, 256, 3072], P(None, None, 'lat', 'lon')
- departures: float32 [393216, 128], P(('lon', 'lat'))
The draws below stay inside these ranges and needn't reach their ends.
Inputs may be any that keep to these rules, and one draw needn't show every extreme that they name: `obs_counts`: each entry counts the live slots of one bucket of 16; slots at or past the count are ignored. In every longitude block some owner latitude block receives full buckets from every source. `obs_columns`: the column within the owner's block, row times 128 plus column. `obs_types`: 0 radiosonde, 1 occultation, 2 radiance.
All inputs are finite; a program needn't handle non-finite values.
Results may differ from the reference program's by a relative error of at most 0.000073.
Values sent between devices are 32-bit elements; how exact they have to be, the bound alone decides.
A program may use at most 32 MiB of HBM per device.

```python
import math
import jax
import jax.numpy as jnp
from jax import lax

FIELDS = 4
LEVELS = 32
LAT_DEV = 8
LON_DEV = 128
SLOTS = 16
STEPS = 4
PROFILE = 128
NLAT = 256
NLON = 3072
ROWS = 393216
N_LON = 24
N_LAT = 32


def draw_obs_counts(key, part):
    key_list = jax.random.split(key, 4)
    grid_shape = (N_LON, N_LAT, N_LAT)
    busy_owner = jax.random.randint(key_list[0], (N_LON, 1, N_LAT), 0, 2)
    full_owner = jax.random.randint(key_list[1], (N_LON, 1, 1), 0, N_LAT)
    high_draw = jax.random.randint(key_list[2], grid_shape, 0, SLOTS + 1)
    low_draw = jax.random.randint(key_list[3], grid_shape, 0, SLOTS * 3 // 4 + 1)
    owner_index = jnp.arange(N_LAT, dtype=jnp.int32).reshape(1, 1, N_LAT)
    counted = jnp.where(busy_owner == 1, high_draw, low_draw)
    counted = jnp.where(owner_index == full_owner, SLOTS, counted)
    return counted.reshape(-1).astype(jnp.int32)


def place_ends(values, own_key, smallest, high):
    longest = values.shape.index(max(values.shape))
    spots = []
    for shift in (0, 1):
        where = [jax.random.randint(jax.random.fold_in(own_key, axis), (), 0, length) for axis, length in enumerate(values.shape)]
        where[longest] = (where[longest] + shift) % values.shape[longest]
        spots.append(tuple(where))
    return values.at[spots[0]].set(smallest).at[spots[1]].set(high)


def block_scale(stream_key, extent, shards, smallest, top_value):
    level, own = 1.0, jax.random.fold_in(stream_key, 6)
    for dim, blocks in shards:
        steps = jnp.exp(jax.random.uniform(jax.random.fold_in(own, dim), (blocks,), jnp.float32, smallest / len(shards), top_value / len(shards)))
        level = level * jnp.repeat(steps, extent[dim] // blocks).reshape([-1 if axis == dim else 1 for axis in range(len(extent))])
    return level


def normal_values(stream_key, shape, width, limit, cuts=(), kind=jnp.bfloat16):
    level = block_scale(stream_key, shape, cuts, -0.22, 0.18) if cuts else 1.0
    drawn = jax.random.normal(stream_key, shape, jnp.float32) * width * level
    return jnp.minimum(jnp.maximum(drawn, -limit), limit).astype(kind)


def setup_inputs(seed: int = 0) -> dict:
    arg_keys = jax.random.split(jax.random.key(seed), 10)
    return {
        "increment": normal_values(arg_keys[0], (FIELDS, LEVELS, NLAT, NLON), 1.0, 6.0, ((2, 32), (3, 24)), jnp.float32),
        "coef_lon": jnp.clip(0.4 + 0.09 * jax.random.uniform(arg_keys[1], (FIELDS, NLAT, NLON), jnp.float32) ** block_scale(arg_keys[1], (FIELDS, NLAT, NLON), ((1, 32), (2, 24)), -0.2, 0.2), 0.4, 0.49),
        "coef_lat": jnp.clip(0.4 + 0.09 * jax.random.uniform(arg_keys[2], (FIELDS, NLAT, NLON), jnp.float32) ** block_scale(arg_keys[2], (FIELDS, NLAT, NLON), ((1, 32), (2, 24)), -0.2, 0.2), 0.4, 0.49),
        "obs_values": normal_values(arg_keys[3], (ROWS, PROFILE), 0.3, 1.8, ((0, 768),), jnp.float32),
        "obs_weight": jnp.clip(jnp.exp(math.log(4.0) - 2.7725887 * jax.random.uniform(arg_keys[4], (ROWS, PROFILE), jnp.float32) ** block_scale(arg_keys[4], (ROWS, PROFILE), ((0, 768),), -0.2, 0.2)), 0.25, 4.0),
        "obs_operator": normal_values(arg_keys[5], (3, PROFILE, PROFILE), PROFILE ** -0.5, 0.5, (), jnp.float32),
        "obs_columns": place_ends(jax.random.randint(arg_keys[6], (ROWS,), 0, LAT_DEV * LON_DEV), jax.random.fold_in(arg_keys[6], 1), 0, (LAT_DEV * LON_DEV) - 1).astype(jnp.int32),
        "obs_types": place_ends(jax.random.randint(arg_keys[7], (ROWS,), 0, 3), jax.random.fold_in(arg_keys[7], 1), 0, 2).astype(jnp.int32),
        "obs_counts": draw_obs_counts(jax.random.fold_in(arg_keys[9], 71), 0),
    }


def spread_field(field_state, root_lon, root_lat, sign_value):
    scaled_lon = root_lon * field_state
    second_lon = jnp.roll(scaled_lon, -1, 2) + jnp.roll(scaled_lon, 1, 2) - 2.0 * scaled_lon
    scaled_lat = root_lat * field_state
    mirrored = jnp.roll(scaled_lat, NLON // 2, 2) * sign_value
    north_side = jnp.concatenate([scaled_lat[:, 1:, :], mirrored[:, -1:, :]], 1)
    south_side = jnp.concatenate([mirrored[:, :1, :], scaled_lat[:, :-1, :]], 1)
    second_lat = north_side + south_side - 2.0 * scaled_lat
    return field_state + root_lon * second_lon + root_lat * second_lat


def diffuse(grid_state, coef_lon, coef_lat):
    sign_table = jnp.array([1.0, 1.0, -1.0, -1.0], jnp.float32)

    def per_field(packed):
        field_state, root_lon, root_lat, sign_value = packed
        for turn in range(STEPS):
            field_state = spread_field(field_state, root_lon[None], root_lat[None], sign_value)
        return field_state

    return lax.map(per_field, (grid_state, coef_lon, coef_lat, sign_table))


def reference(increment, coef_lon, coef_lat, obs_values, obs_weight, obs_operator, obs_columns, obs_types, obs_counts):
    highest = lax.Precision.HIGHEST
    state = diffuse(increment, coef_lon, coef_lat)
    counts_grid = obs_counts.reshape(N_LON, N_LAT, N_LAT, 1)
    slot_index = jnp.arange(SLOTS, dtype=jnp.int32).reshape(1, 1, 1, SLOTS)
    live = (slot_index < counts_grid).reshape(-1)
    local_col = obs_columns.reshape(N_LON, N_LAT, N_LAT, SLOTS)
    owner_lat = jnp.arange(N_LAT, dtype=jnp.int32).reshape(1, 1, N_LAT, 1)
    source_lon = jnp.arange(N_LON, dtype=jnp.int32).reshape(N_LON, 1, 1, 1)
    grid_row = owner_lat * LAT_DEV + local_col // LON_DEV
    grid_col = source_lon * LON_DEV + local_col % LON_DEV
    flat_cell = (grid_row * NLON + grid_col).reshape(-1).astype(jnp.int32)
    flat_state = state.reshape(PROFILE, NLAT * NLON)
    columns = flat_state[:, flat_cell].T
    model_all = [jnp.dot(columns, obs_operator[kind], precision=highest) for kind in range(3)]
    model = jnp.where((obs_types == 0)[:, None], model_all[0], jnp.where((obs_types == 1)[:, None], model_all[1], model_all[2]))
    departures = jnp.where(live[:, None], obs_values - model, jnp.float32(0.0))
    weighted = obs_weight * departures
    adjoint_all = [jnp.dot(weighted, obs_operator[kind].T, precision=highest) for kind in range(3)]
    adjoint = jnp.where((obs_types == 0)[:, None], adjoint_all[0], jnp.where((obs_types == 1)[:, None], adjoint_all[1], adjoint_all[2]))
    forcing = jnp.zeros((PROFILE, NLAT * NLON), jnp.float32).at[:, flat_cell].add(adjoint.T)
    smoothed = diffuse(forcing.reshape(FIELDS, LEVELS, NLAT, NLON), coef_lon, coef_lat)
    return increment - smoothed, departures
```

```python
import functools

import jax
import jax.numpy as jnp
from jax import lax
from jax.experimental import pallas as pl
from jax.experimental.pallas import tpu as pltpu
from jax.sharding import PartitionSpec as P

HALO = 4
STEPS = 4
ROWS = 8
EXT = ROWS + 2 * HALO
LANES = 128
FIELDS = 4
PROFILE = 128
GROUPS = PROFILE // 8
KINDS = 3
F32 = jnp.float32
BF16 = jnp.bfloat16


def lane_iota(shape):
    return lax.broadcasted_iota(jnp.int32, shape, len(shape) - 1)


def split(x):
    hi = x.astype(BF16)
    return hi, (x - hi.astype(F32)).astype(BF16)


def kernel(
    n_lon, n_lat, slots,
    inc_h, clon_h, clat_h, obs_h, wgt_h, op_h, col_h, typ_h, cnt_h,
    grad_o, dep_o,
    inc_v, cf_v, op_v, col_v, typ_v, cnt_v, obs_v, wgt_v, code_v, codes_in, codet_v, dep_v, out_v,
    xa, pa, xe, pe, coefs, strips, edges, state_v, st_v, oh_v, opf_v, opb_v, lhs_hi, lhs_lo, adj_v,
    load_sem, own_sem, send_sem, recv_row, recv_corner, recv_side, a2a_send, a2a_recv,
):
    lon, lat = lax.axis_index("lon"), lax.axis_index("lat")
    n_rows = n_lat * slots
    tiles = n_rows // LANES
    per_tile = LANES // slots
    south, north = lat == 0, lat == n_lat - 1
    south_i, north_i = south.astype(jnp.int32), north.astype(jnp.int32)
    opposite = n_lon // 2

    def lon_at(by):
        return lax.rem(lon + by + n_lon, n_lon)

    def prev_of(d):
        return (lon_at(d + opposite * south_i), lat - 1 + south_i)

    def next_of(d):
        return (lon_at(d + opposite * north_i), lat + 1 - north_i)

    def dev(where):
        return {"lon": where[0], "lat": where[1]}

    barrier = pltpu.get_barrier_semaphore()

    def greet(where):
        pl.semaphore_signal(barrier, inc=1, device_id=dev(where), device_id_type=pl.DeviceIdType.MESH)

    for d in (-1, 1):
        greet(prev_of(d))
        greet(next_of(d))
        greet((lon_at(d), lat))

    @pl.when(south)
    def _():
        greet(prev_of(0))

    @pl.when(north)
    def _():
        greet(next_of(0))

    @pl.loop(1, n_lat)
    def _(k):
        greet((lon, lax.rem(lat + k, n_lat)))

    loads = [
        pltpu.make_async_copy(src, dst, load_sem.at[i])
        for i, (src, dst) in enumerate(
            (
                (inc_h, inc_v), (clon_h, cf_v.at[0]), (clat_h, cf_v.at[1]), (op_h, op_v),
                (col_h, col_v), (typ_h, typ_v), (cnt_h, cnt_v),
            )
        )
    ]
    for load in loads:
        load.start()
    mine = pl.ds(pl.multiple_of(lat * slots, slots), slots)
    own = [
        pltpu.make_async_copy(obs_h.at[mine], obs_v.at[mine], own_sem.at[0]),
        pltpu.make_async_copy(wgt_h.at[mine], wgt_v.at[mine], own_sem.at[1]),
    ]
    for copy in own:
        copy.start()
    lane = lane_iota((8, LANES))
    slot_of = lane >> 3
    in_slot = lane & 7

    for i in (4, 5, 6):
        loads[i].wait()
    rep = (lane_iota((n_lat, n_rows)) // slots == lax.broadcasted_iota(jnp.int32, (n_lat, n_rows), 0)).astype(F32).astype(BF16)
    counts = jnp.broadcast_to(cnt_v[...].astype(F32), (8, n_lat)).astype(BF16)
    limit = jnp.dot(counts, rep, preferred_element_type=F32)
    for q in range(tiles):
        lim = limit[0:1, q * LANES : (q + 1) * LANES].astype(jnp.int32)
        code = col_v[q : q + 1, :] * 4 + typ_v[q : q + 1, :] + 1
        code_v[q] = jnp.where(lane_iota((1, LANES)) % slots < lim, code, 0)

    def pack(v):
        packed = jnp.zeros((8, LANES), F32)
        for s in range(GROUPS):
            packed = jnp.where(slot_of == s, pltpu.roll(v(s), 8 * s + HALO, 1), packed)
        return packed

    for i in (0, 1, 2):
        loads[i].wait()

    @pl.loop(0, ROWS)
    def _(r):
        for s in range(GROUPS):
            xa[r + HALO, s * 8 : (s + 1) * 8, :] = inc_v[pl.ds(s * 64 + r, 8, stride=8), :]
        for ct in range(2):
            xa[r + HALO, PROFILE + ct * 4 : PROFILE + ct * 4 + 4, :] = cf_v[ct, pl.ds(r, 4, stride=8), :]
        pa[1, r + HALO, 0:8, :] = pack(lambda s: xa[r + HALO, s * 8 : (s + 1) * 8, :])
        both = xa[r + HALO, PROFILE : PROFILE + 8, :]
        table = pack(lambda s: both)
        for ct in range(2):
            coef = jnp.zeros((8, LANES), F32)
            for f in range(FIELDS):
                coef = jnp.where(slot_of >> 2 == f, jnp.broadcast_to(table[ct * 4 + f : ct * 4 + f + 1, :], (8, LANES)), coef)
            pa[1, r + HALO, 8 + ct * 8 : 16 + ct * 8, :] = coef

    def expand(r):
        for f in range(FIELDS):
            a = jnp.broadcast_to(xa[r, PROFILE + f : PROFILE + f + 1, :], (8, LANES))
            b = jnp.broadcast_to(xa[r, PROFILE + 4 + f : PROFILE + 5 + f, :], (8, LANES))
            coefs[0, r, f] = a
            coefs[1, r, f] = b
            coefs[2, r, f] = 1.0 - 2.0 * (a * a + b * b)

    pl.semaphore_wait(barrier, n_lat - 1 + 6 + south_i + north_i)

    low, high = pl.ds(HALO, HALO), pl.ds(2 * HALO, HALO)
    to_prev = pl.ds(3 * HALO * (1 - south_i), HALO)
    to_next = pl.ds(3 * HALO * north_i, HALO)
    prev_side, next_side = 1 - south_i, north_i

    def exchange(phase, x, p):
        def send(i, src, dst, sem, where):
            return pltpu.make_async_remote_copy(
                src_ref=src, dst_ref=dst, send_sem=send_sem.at[phase, i], recv_sem=sem,
                device_id=dev(where), device_id_type=pl.DeviceIdType.MESH,
            )

        copies = [
            send(0, x.at[low], x.at[to_prev], recv_row.at[phase, prev_side], prev_of(0)),
            send(1, x.at[high], x.at[to_next], recv_row.at[phase, next_side], next_of(0)),
        ]
        own_rows = pl.ds(HALO, ROWS)
        for i, d in enumerate((-1, 1)):
            copies.append(send(2 + i, p.at[1, own_rows], p.at[1 - d, own_rows], recv_side.at[phase, i], (lon_at(d), lat)))
        for i, d in enumerate((-1, 0, 1)):
            copies.append(send(4 + i, p.at[1, low], p.at[1 - d, to_prev], recv_corner.at[phase, prev_side, i], prev_of(d)))
            copies.append(send(7 + i, p.at[1, high], p.at[1 - d, to_next], recv_corner.at[phase, next_side, i], next_of(d)))
        return copies

    def settle(phase, x, p):
        def arrive(ref, sem):
            pltpu.make_async_copy(ref, ref, sem).wait()

        own_rows = pl.ds(HALO, ROWS)
        for i, d in enumerate((-1, 1)):
            arrive(p.at[1 - d, own_rows], recv_side.at[phase, i])
        for side, rows in enumerate((pl.ds(0, HALO), pl.ds(3 * HALO, HALO))):
            for i, d in enumerate((-1, 0, 1)):
                arrive(p.at[1 - d, rows], recv_corner.at[phase, side, i])
            arrive(x.at[rows], recv_row.at[phase, side])

    first = exchange(0, xa, pa)
    for copy in first:
        copy.start()

    @pl.loop(1, n_lat)
    def _(k):
        to = lax.rem(lat + k, n_lat)
        pltpu.make_async_remote_copy(
            src_ref=code_v.at[to // per_tile], dst_ref=codes_in.at[lat], send_sem=a2a_send.at[0], recv_sem=a2a_recv.at[0],
            device_id=dev((lon, to)), device_id_type=pl.DeviceIdType.MESH,
        ).start()

    @pl.loop(1, n_lat)
    def _(k):
        to = lax.rem(lat + k, n_lat)
        theirs = pl.ds(pl.multiple_of(to * slots, slots), slots)
        for i, (src, dst) in enumerate(((obs_h, obs_v), (wgt_h, wgt_v))):
            pltpu.make_async_remote_copy(
                src_ref=src.at[theirs], dst_ref=dst.at[mine], send_sem=a2a_send.at[1 + i], recv_sem=a2a_recv.at[1 + i],
                device_id=dev((lon, to)), device_id_type=pl.DeviceIdType.MESH,
            ).start()

    def all_but_one(ref, sem):
        part = ref.at[pl.ds(0, ref.shape[0] // n_lat * (n_lat - 1))]
        pltpu.make_async_copy(part, part, sem).wait()

    loads[3].wait()
    for k in range(KINDS):
        hi, lo = split(op_v[k])
        opf_v[k * PROFILE : (k + 1) * PROFILE, :] = jnp.concatenate([hi, lo], 1)
        hi, lo = split(jnp.transpose(op_v[k]))
        opb_v[k * PROFILE : (k + 1) * PROFILE, :] = jnp.concatenate([hi, lo], 1)

    @pl.loop(HALO, HALO + ROWS)
    def _(r):
        expand(r)

    all_but_one(codes_in, a2a_recv.at[0])
    codes_in[lat] = code_v[lat // per_tile]
    mod = lax.rem(lat, per_tile)
    lane_1 = lane_iota((1, LANES))
    for q in range(tiles):
        row = jnp.zeros((1, LANES), jnp.int32)
        for j in range(per_tile):
            moved = pltpu.roll(codes_in[q * per_tile + j], lax.rem(LANES + slots * (j - mod), LANES), 1)
            row = jnp.where(lane_1 // slots == j, moved, row)
        turned = jnp.transpose(jnp.broadcast_to(row.astype(F32), (LANES, LANES))).astype(jnp.int32)
        codet_v[q * LANES : (q + 1) * LANES, :] = turned
        cell = (turned - 1) >> 2
        for r in range(ROWS):
            hit = cell == lane_iota((LANES, LANES)) + r * LANES
            oh_v[q * LANES : (q + 1) * LANES, r * LANES : (r + 1) * LANES] = jnp.where(hit, 1.0, 0.0).astype(BF16)

    sign_south = jnp.where(south, -1.0, 1.0).astype(F32)
    sign_north = jnp.where(north, -1.0, 1.0).astype(F32)
    def row_at(r):
        if r < HALO:
            return r + (HALO - 1 - 2 * r) * south_i
        if r >= HALO + ROWS:
            j = r - HALO - ROWS
            return r + (HALO - 1 - 2 * j) * north_i
        return r

    def sign_at(r):
        return sign_south if r < HALO else sign_north if r >= HALO + ROWS else None

    def merged(p, r, part):
        at = row_at(r)
        rows = slice(part * 8, part * 8 + 8)
        west, mid, east = p[0, at, rows, :], p[1, at, rows, :], p[2, at, rows, :]
        return jnp.where(in_slot < HALO, west, mid), jnp.where(in_slot < HALO, mid, east)

    def evolve_strips(p):
        cur = [[None] * EXT, [None] * EXT]
        for r in range(EXT):
            w, z = merged(p, r, 0)
            if sign_at(r) is not None:
                sign = jnp.where(lane >= 64, sign_at(r), 1.0)
                w, z = w * sign, z * sign
            cur[0][r], cur[1][r] = w, z
        for t in range(STEPS):
            inner = range(t + 1, EXT - 1 - t)
            g = [{}, {}]
            for side in range(2):
                for r in inner:
                    g[side][r] = strips[side, 0, r] * cur[side][r]
            for r in inner:
                edges[t, r] = jnp.where(in_slot == 2, pltpu.roll(g[1][r], LANES - 2, 1), g[0][r])
            if t < STEPS - 1:
                for side in range(2):
                    h = {r: strips[side, 1, r] * cur[side][r] for r in range(t, EXT - t)}
                    new = [None] * EXT
                    for r in inner:
                        gr = g[side][r]
                        new[r] = (
                            strips[side, 2, r] * cur[side][r]
                            + strips[side, 0, r] * (pltpu.roll(gr, 1, 1) + pltpu.roll(gr, LANES - 1, 1))
                            + strips[side, 1, r] * (h[r - 1] + h[r + 1])
                        )
                    cur[side] = new

    def diffuse(x, give):
        @pl.loop(0, GROUPS)
        def _(s):
            f = s // 4
            rows = pl.ds(pl.multiple_of(s * 8, 8), 8)
            wind = s >= GROUPS // 2
            flip_s = jnp.where(wind, sign_south, 1.0)
            flip_n = jnp.where(wind, sign_north, 1.0)
            turn = LANES - HALO + 1 - 8 * s
            cur = []
            for r in range(EXT):
                v = x[row_at(r), rows, :]
                if r < HALO:
                    v = v * flip_s
                if r >= HALO + ROWS:
                    v = v * flip_n
                cur.append(v)
            for t in range(STEPS):
                h = {r: coefs[1, r, f] * cur[r] for r in range(t, EXT - t)}
                new = [None] * EXT
                for r in range(t + 1, EXT - 1 - t):
                    a = coefs[0, r, f]
                    g = a * cur[r]
                    e = pltpu.roll(edges[t, r], turn, 1)
                    lateral = jnp.where(lane == 0, e, pltpu.roll(g, 1, 1)) + jnp.where(lane == LANES - 1, e, pltpu.roll(g, LANES - 1, 1))
                    new[r] = coefs[2, r, f] * cur[r] + a * lateral + coefs[1, r, f] * (h[r - 1] + h[r + 1])
                cur = new
            for r in range(ROWS):
                give(r, s, cur[r + HALO])

    settle(0, xa, pa)
    for r in range(EXT):
        for ct in range(2):
            w, z = merged(pa, r, 1 + ct)
            strips[0, ct, r], strips[1, ct, r] = w, z
        for side in range(2):
            a, b = strips[side, 0, r], strips[side, 1, r]
            strips[side, 2, r] = 1.0 - 2.0 * (a * a + b * b)
    for r in list(range(HALO)) + list(range(HALO + ROWS, EXT)):
        at = row_at(r)
        for f in range(FIELDS):
            a = jnp.broadcast_to(xa[at, PROFILE + f : PROFILE + f + 1, :], (8, LANES))
            b = jnp.broadcast_to(xa[at, PROFILE + 4 + f : PROFILE + 5 + f, :], (8, LANES))
            coefs[0, r, f] = a
            coefs[1, r, f] = b
            coefs[2, r, f] = 1.0 - 2.0 * (a * a + b * b)
    evolve_strips(pa)

    def keep_state(r, s, v):
        state_v[r, pl.ds(pl.multiple_of(s * 8, 8), 8), :] = v

    diffuse(xa, keep_state)

    for r in range(ROWS):
        hi, lo = split(jnp.transpose(state_v[r]))
        st_v[r * LANES : (r + 1) * LANES, :] = jnp.concatenate([hi, lo], 1)
    found = jnp.dot(oh_v[...], st_v[...], preferred_element_type=F32)
    columns = found[:, :PROFILE] + found[:, PROFILE:]

    def by_kind(values, table):
        hi, lo = split(values)
        kind = codet_v[...]
        kind = (kind - 1) & 3
        for k in range(KINDS):
            of_kind = kind == k
            lhs_hi[:, k * PROFILE : (k + 1) * PROFILE] = jnp.where(of_kind, hi.astype(F32), 0.0).astype(BF16)
            lhs_lo[:, k * PROFILE : (k + 1) * PROFILE] = jnp.where(of_kind, lo.astype(F32), 0.0).astype(BF16)
        one = jnp.dot(lhs_hi[...], table[...], preferred_element_type=F32)
        two = jnp.dot(lhs_lo[...], table[:, :PROFILE], preferred_element_type=F32)
        return one[:, :PROFILE] + one[:, PROFILE:] + two

    model = by_kind(columns, opf_v)
    for copy in own:
        copy.wait()
    all_but_one(obs_v, a2a_recv.at[1])
    all_but_one(wgt_v, a2a_recv.at[2])
    dep = jnp.where(codet_v[...] > 0, obs_v[...] - model, 0.0)
    dep_v[...] = dep
    adj = by_kind(wgt_v[...] * dep, opb_v)
    hi, lo = split(jnp.transpose(adj))
    adj_v[0:PROFILE, :] = hi
    adj_v[PROFILE : 2 * PROFILE, :] = lo
    for part in range(2):
        spread = jnp.dot(adj_v[...], oh_v[:, part * 4 * LANES : (part + 1) * 4 * LANES], preferred_element_type=F32)
        for r in range(4):
            xe[HALO + part * 4 + r] = spread[:PROFILE, r * LANES : (r + 1) * LANES] + spread[PROFILE:, r * LANES : (r + 1) * LANES]

    @pl.loop(HALO, HALO + ROWS)
    def _(r):
        pe[1, r] = pack(lambda s: xe[r, s * 8 : (s + 1) * 8, :])

    second = exchange(1, xe, pe)
    for copy in second:
        copy.start()

    back = pltpu.make_async_copy(dep_v.at[mine], dep_o.at[mine], own_sem.at[2])
    back.start()

    @pl.loop(1, n_lat)
    def _(k):
        to = lax.rem(lat + k, n_lat)
        theirs = pl.ds(pl.multiple_of(to * slots, slots), slots)
        pltpu.make_async_remote_copy(
            src_ref=dep_v.at[theirs], dst_ref=dep_o.at[mine], send_sem=a2a_send.at[3], recv_sem=a2a_recv.at[3],
            device_id=dev((lon, to)), device_id_type=pl.DeviceIdType.MESH,
        ).start()

    settle(1, xe, pe)
    evolve_strips(pe)

    def keep_gradient(r, s, v):
        rows = pl.ds(s * 64 + r, 8, stride=8)
        out_v[rows, :] = inc_v[rows, :] - v

    diffuse(xe, keep_gradient)
    last = pltpu.make_async_copy(out_v, grad_o, load_sem.at[0])
    last.start()

    for copy in first + second:
        copy.wait_send()
    all_but_one(codes_in, a2a_send.at[0])
    all_but_one(obs_v, a2a_send.at[1])
    all_but_one(wgt_v, a2a_send.at[2])
    all_but_one(dep_v, a2a_send.at[3])
    all_but_one(dep_o, a2a_recv.at[3])
    back.wait()
    last.wait()


def local(n_lon, n_lat, increment, coef_lon, coef_lat, obs_values, obs_weight, obs_operator, obs_columns, obs_types, obs_counts):
    n_rows = obs_columns.shape[0]
    slots = n_rows // n_lat
    tiles = n_rows // LANES
    cells = ROWS * LANES
    any_spec = pl.BlockSpec(memory_space=pl.ANY)
    gradient, departures = pl.pallas_call(
        functools.partial(kernel, n_lon, n_lat, slots),
        out_shape=(
            jax.ShapeDtypeStruct((PROFILE * ROWS, LANES), F32),
            jax.ShapeDtypeStruct((n_rows, PROFILE), F32),
        ),
        in_specs=[any_spec] * 9,
        out_specs=(any_spec, any_spec),
        scratch_shapes=[
            pltpu.VMEM((PROFILE * ROWS, LANES), F32),
            pltpu.VMEM((2, FIELDS * ROWS, LANES), F32),
            pltpu.VMEM((KINDS, PROFILE, PROFILE), F32),
            pltpu.VMEM((tiles, LANES), jnp.int32),
            pltpu.VMEM((tiles, LANES), jnp.int32),
            pltpu.VMEM((1, n_lat), jnp.int32),
            pltpu.VMEM((n_rows, PROFILE), F32),
            pltpu.VMEM((n_rows, PROFILE), F32),
            pltpu.VMEM((tiles, 1, LANES), jnp.int32),
            pltpu.VMEM((n_lat, 1, LANES), jnp.int32),
            pltpu.VMEM((n_rows, LANES), jnp.int32),
            pltpu.VMEM((n_rows, PROFILE), F32),
            pltpu.VMEM((PROFILE * ROWS, LANES), F32),
            pltpu.VMEM((EXT, PROFILE + 8, LANES), F32),
            pltpu.VMEM((3, EXT, 24, LANES), F32),
            pltpu.VMEM((EXT, PROFILE, LANES), F32),
            pltpu.VMEM((3, EXT, 8, LANES), F32),
            pltpu.VMEM((3, EXT, FIELDS, 8, LANES), F32),
            pltpu.VMEM((2, 3, EXT, 8, LANES), F32),
            pltpu.VMEM((STEPS, EXT, 8, LANES), F32),
            pltpu.VMEM((ROWS, PROFILE, LANES), F32),
            pltpu.VMEM((cells, 2 * PROFILE), BF16),
            pltpu.VMEM((n_rows, cells), BF16),
            pltpu.VMEM((KINDS * PROFILE, 2 * PROFILE), BF16),
            pltpu.VMEM((KINDS * PROFILE, 2 * PROFILE), BF16),
            pltpu.VMEM((n_rows, KINDS * PROFILE), BF16),
            pltpu.VMEM((n_rows, KINDS * PROFILE), BF16),
            pltpu.VMEM((2 * PROFILE, n_rows), BF16),
            pltpu.SemaphoreType.DMA((7,)),
            pltpu.SemaphoreType.DMA((3,)),
            pltpu.SemaphoreType.DMA((2, 10)),
            pltpu.SemaphoreType.DMA((2, 2)),
            pltpu.SemaphoreType.DMA((2, 2, 3)),
            pltpu.SemaphoreType.DMA((2, 2)),
            pltpu.SemaphoreType.DMA((4,)),
            pltpu.SemaphoreType.DMA((4,)),
        ],
        compiler_params=pltpu.CompilerParams(collective_id=0, has_side_effects=True, vmem_limit_bytes=48 * 1024 * 1024),
        name="assimilate",
    )(
        increment.reshape(PROFILE * ROWS, LANES),
        coef_lon.reshape(FIELDS * ROWS, LANES),
        coef_lat.reshape(FIELDS * ROWS, LANES),
        obs_values,
        obs_weight,
        obs_operator,
        obs_columns.reshape(tiles, LANES),
        obs_types.reshape(tiles, LANES),
        obs_counts.reshape(1, n_lat),
    )
    return gradient.reshape(increment.shape), departures


def solution(mesh):
    return jax.shard_map(
        functools.partial(local, mesh.shape["lon"], mesh.shape["lat"]),
        mesh=mesh,
        in_specs=(
            P(None, None, "lat", "lon"),
            P(None, "lat", "lon"),
            P(None, "lat", "lon"),
            P(("lon", "lat"), None),
            P(("lon", "lat"), None),
            P(),
            P(("lon", "lat")),
            P(("lon", "lat")),
            P(("lon", "lat")),
        ),
        out_specs=(P(None, None, "lat", "lon"), P(("lon", "lat"), None)),
        check_vma=False,
    )
```

```python
import functools

import jax
import jax.numpy as jnp
from jax import lax
from jax.experimental import pallas as pl
from jax.experimental.pallas import tpu as pltpu
from jax.sharding import PartitionSpec as P

HALO = 4
STEPS = 4
ROWS = 8
EXT = ROWS + 2 * HALO
LANES = 128
SPAN = LANES // 8
WIDE = SPAN + 2 * HALO
FIELDS = 4
PROFILE = 128
KINDS = 3
F32 = jnp.float32
BF16 = jnp.bfloat16
CORNER = ((1, 0, 3), (2, 3, 2), (3, 5, 1))


def lane_iota(shape):
    return lax.broadcasted_iota(jnp.int32, shape, len(shape) - 1)


def row_iota(shape):
    return lax.broadcasted_iota(jnp.int32, shape, 0)


def split(x):
    hi = x.astype(BF16)
    return hi, (x - hi.astype(F32)).astype(BF16)


def kernel(
    n_lon, n_lat, slots,
    inc_h, clon_h, clat_h, obs_h, wgt_h, op_h, col_h, typ_h, cnt_h,
    grad_o, dep_o,
    inc_v, cf_v, op_v, col_v, typ_v, cnt_v, obs_v, wgt_v, code_v, codes_in, codet_v, dep_v,
    xa, xe, ya, za, turn_v, rows_c, tile_v, tiles_in, side_v, corner_v, from_side, from_corner, relay_v,
    root_a, root_b, mid_c, lon_c, lat_c, st_v, oh_v, oht_v, opf_v, opb_v, lhs_hi, lhs_lo, adj_v,
    load_sem, own_sem, side_send, corner_send, tile_send, row_send, recv_side, recv_corner, recv_tile, recv_row, recv_coef,
    relay_send, relay_recv, a2a_send, a2a_recv,
):
    lon, lat = lax.axis_index("lon"), lax.axis_index("lat")
    n_rows = n_lat * slots
    n_tiles = n_rows // LANES
    per_tile = LANES // slots
    south, north = lat == 0, lat == n_lat - 1
    south_i, north_i = south.astype(jnp.int32), north.astype(jnp.int32)
    opposite = n_lon // 2

    def lon_at(by):
        return lax.rem(lon + by + n_lon, n_lon)

    def prev_of(d):
        return (lon_at(d + opposite * south_i), lat - 1 + south_i)

    def next_of(d):
        return (lon_at(d + opposite * north_i), lat + 1 - north_i)

    last, after = lax.rem(lon, opposite) == opposite - 1, lax.rem(lon, opposite) == 0
    last_i = last.astype(jnp.int32)

    def dev(where):
        return {"lon": where[0], "lat": where[1]}

    barrier = pltpu.get_barrier_semaphore()

    def greet(where):
        pl.semaphore_signal(barrier, inc=1, device_id=dev(where), device_id_type=pl.DeviceIdType.MESH)

    for d in (-1, 1):
        greet(prev_of(d))
        greet(next_of(d))
        greet((lon_at(d), lat))

    @pl.when(south)
    def _():
        greet(prev_of(0))

    @pl.when(north)
    def _():
        greet(next_of(0))

    @pl.when(last)
    def _():
        greet((lon_at(opposite), lat))

    @pl.when(after)
    def _():
        greet((lon_at(opposite - 1), lat))

    @pl.when(after & ~south)
    def _():
        greet((lon_at(opposite - 1), lat - 1))

    @pl.when(after & ~north)
    def _():
        greet((lon_at(opposite - 1), lat + 1))

    @pl.loop(1, n_lat)
    def _(k):
        greet((lon, lax.rem(lat + k, n_lat)))

    loads = [
        pltpu.make_async_copy(src, dst, load_sem.at[i])
        for i, (src, dst) in enumerate(
            (
                (inc_h, inc_v), (clon_h, cf_v.at[0]), (clat_h, cf_v.at[1]), (op_h, op_v),
                (col_h, col_v), (typ_h, typ_v), (cnt_h, cnt_v),
            )
        )
    ]
    for load in loads:
        load.start()
    mine = pl.ds(pl.multiple_of(lat * slots, slots), slots)
    own = [
        pltpu.make_async_copy(obs_h.at[mine], obs_v.at[mine], own_sem.at[0]),
        pltpu.make_async_copy(wgt_h.at[mine], wgt_v.at[mine], own_sem.at[1]),
    ]
    for copy in own:
        copy.start()

    for i in (4, 5, 6):
        loads[i].wait()
    rep = (lane_iota((n_lat, n_rows)) // slots == row_iota((n_lat, n_rows))).astype(F32).astype(BF16)
    counts = jnp.broadcast_to(cnt_v[...].astype(F32), (8, n_lat)).astype(BF16)
    limit = jnp.dot(counts, rep, preferred_element_type=F32)
    for q in range(n_tiles):
        lim = limit[0:1, q * LANES : (q + 1) * LANES].astype(jnp.int32)
        code = col_v[q : q + 1, :] * 4 + typ_v[q : q + 1, :] + 1
        code_v[q] = jnp.where(lane_iota((1, LANES)) % slots < lim, code, 0)

    for i in (0, 1, 2):
        loads[i].wait()

    @pl.loop(0, ROWS)
    def _(r):
        turn_v[r] = jnp.transpose(inc_v[pl.ds(r, PROFILE, stride=ROWS), :])
        for i in range(SPAN):
            xa[r + HALO, HALO + i] = turn_v[r, pl.ds(i, 8, stride=SPAN), :]
        for ct in range(2):
            rows_c[r + HALO, ct * FIELDS : (ct + 1) * FIELDS, :] = cf_v[ct, pl.ds(r, FIELDS, stride=ROWS), :]

    first, end = HALO, HALO + SPAN

    def stage(phase, x):
        for r in range(ROWS):
            for j in range(HALO):
                at = r % 2 * HALO + j
                side_v[phase, 0, r // 2, at : at + 1, :] = x[r + HALO, end - HALO + j, 7:8, :]
                side_v[phase, 1, r // 2, at : at + 1, :] = x[r + HALO, first + j, 0:1, :]
        for half in range(2):
            for k, at, n in CORNER:
                r = HALO + k - 1 if half == 0 else HALO + ROWS - k
                for j in range(n):
                    corner_v[phase, half, 0, at + j : at + j + 1, :] = x[r, end - n + j, 7:8, :]
                    corner_v[phase, half, 1, at + j : at + j + 1, :] = x[r, first + j, 0:1, :]

    stage(0, xa)
    lane = lane_iota((8, LANES))
    tile = jnp.zeros((8, LANES), F32)
    for r in range(ROWS):
        v = rows_c[r + HALO]
        tile = jnp.where(lane >> 2 == r, pltpu.roll(v, 4 * r + HALO, 1), tile)
        tile = jnp.where(lane >> 2 == r + 16, pltpu.roll(v, 64 + 4 * r, 1), tile)
    tile_v[0] = tile

    pl.semaphore_wait(barrier, n_lat - 1 + 6 + south_i + north_i + last_i * (4 - south_i - north_i))

    low, high = pl.ds(HALO, HALO), pl.ds(2 * HALO, HALO)
    inner = pl.ds(HALO, SPAN)
    to_prev = pl.ds(3 * HALO * (1 - south_i), HALO)
    to_next = pl.ds(3 * HALO * north_i, HALO)
    prev_side, next_side = 1 - south_i, north_i

    def send(src, dst, send_at, sem, where):
        return pltpu.make_async_remote_copy(
            src_ref=src, dst_ref=dst, send_sem=send_at, recv_sem=sem,
            device_id=dev(where), device_id_type=pl.DeviceIdType.MESH,
        )

    def start(copies):
        for copy in copies:
            copy.start()
        return copies

    class Routed:
        def __init__(self, other, plain, changed):
            self.other, self.plain, self.changed = other, plain, changed

        def start(self):
            pl.when(self.other)(self.changed.start)
            pl.when(~self.other)(self.plain.start)

        def wait_send(self):
            self.plain.wait_send()

    def by_relay(part, src, send_at):
        at = relay_v.at[pl.ds(*((0, 4), (4, 1), (5, 1), (6, 1))[part])]
        return send(src, at, send_at, relay_recv.at[part], (lon_at(opposite), lat))

    def small_copies(phase):
        copies = []
        for i, d in enumerate((1, -1)):
            src, send_at = side_v.at[phase, i], side_send.at[phase, i]
            copy = send(src, from_side.at[phase, i], send_at, recv_side.at[phase], (lon_at(d), lat))
            copies.append(copy if i or phase else Routed(last, copy, by_relay(0, src, send_at)))
            for half, side, where, pole in ((0, prev_side, prev_of(d), south), (1, next_side, next_of(d), north)):
                src, send_at = corner_v.at[phase, half, pl.ds(i, 1)], corner_send.at[phase, half, i]
                copy = send(src, from_corner.at[phase, side, pl.ds(i, 1)], send_at, recv_corner.at[phase], where)
                copies.append(copy if i or phase else Routed(last & ~pole, copy, by_relay(1 + half, src, send_at)))
        return copies

    def tile_copies():
        copies = []
        for i, d in enumerate((1, -1)):
            for v, (at, where, pole) in enumerate(
                ((2, (lon_at(d), lat), None), (prev_side, prev_of(d), south), (next_side, next_of(d), north))
            ):
                copy = send(tile_v, tiles_in.at[at, pl.ds(i, 1)], tile_send.at[v, i], recv_tile, where)
                if i == 0 and v == 0:
                    copy = Routed(last, copy, by_relay(3, tile_v, tile_send.at[v, i]))
                copies.append(copy if i or not v else Only(~last | pole, copy))
        return copies

    class Only:
        def __init__(self, holds, copy):
            self.holds, self.copy = holds, copy

        def start(self):
            pl.when(self.holds)(self.copy.start)

        def wait_send(self):
            pl.when(self.holds)(self.copy.wait_send)

    def pass_on():
        over = lon_at(1 - opposite)
        ways = [
            (last, 0, (0, 4), from_side.at[0, 0], recv_side.at[0], lat),
            (last & ~south, 1, (4, 1), from_corner.at[0, 1, pl.ds(0, 1)], recv_corner.at[0], lat - 1),
            (last & ~north, 2, (5, 1), from_corner.at[0, 0, pl.ds(0, 1)], recv_corner.at[0], lat + 1),
            (last, 3, (6, 1), tiles_in.at[2, pl.ds(0, 1)], recv_tile, lat),
            (last & ~south, None, (6, 1), tiles_in.at[1, pl.ds(0, 1)], recv_tile, lat - 1),
            (last & ~north, None, (6, 1), tiles_in.at[0, pl.ds(0, 1)], recv_tile, lat + 1),
        ]
        copies = []
        for n, (holds, part, (at, count), dst, sem, to) in enumerate(ways):
            src = relay_v.at[pl.ds(at, count)]
            copy = Only(holds, send(src, dst, relay_send.at[n], sem, (over, to)))
            if part is not None:
                arrived = pltpu.make_async_copy(src, src, relay_recv.at[part])
                pl.when(holds)(arrived.wait)
            copy.start()
            copies.append(copy)
        return copies

    def row_copies(phase, x):
        return [
            send(x.at[low, inner], x.at[to_prev, inner], row_send.at[phase, 0], recv_row.at[phase, prev_side], prev_of(0)),
            send(x.at[high, inner], x.at[to_next, inner], row_send.at[phase, 1], recv_row.at[phase, next_side], next_of(0)),
        ]

    def coef_copies():
        return [
            send(rows_c.at[low], rows_c.at[to_prev], row_send.at[2, 0], recv_coef.at[prev_side], prev_of(0)),
            send(rows_c.at[high], rows_c.at[to_next], row_send.at[2, 1], recv_coef.at[next_side], next_of(0)),
        ]

    def arrive(ref, sem):
        pltpu.make_async_copy(ref, ref, sem).wait()

    sent = start(small_copies(0) + tile_copies() + coef_copies())

    @pl.loop(1, n_lat)
    def _(k):
        to = lax.rem(lat + k, n_lat)
        pltpu.make_async_remote_copy(
            src_ref=code_v.at[to // per_tile], dst_ref=codes_in.at[lat], send_sem=a2a_send.at[0], recv_sem=a2a_recv.at[0],
            device_id=dev((lon, to)), device_id_type=pl.DeviceIdType.MESH,
        ).start()

    sent += start(row_copies(0, xa))

    @pl.loop(1, n_lat)
    def _(k):
        to = lax.rem(lat + k, n_lat)
        theirs = pl.ds(pl.multiple_of(to * slots, slots), slots)
        for i, (src, dst) in enumerate(((obs_h, obs_v), (wgt_h, wgt_v))):
            pltpu.make_async_remote_copy(
                src_ref=src.at[theirs], dst_ref=dst.at[mine], send_sem=a2a_send.at[1 + i], recv_sem=a2a_recv.at[1 + i],
                device_id=dev((lon, to)), device_id_type=pl.DeviceIdType.MESH,
            ).start()

    def all_but_one(ref, sem):
        part = ref.at[pl.ds(0, ref.shape[0] // n_lat * (n_lat - 1))]
        pltpu.make_async_copy(part, part, sem).wait()

    sent += pass_on()
    loads[3].wait()
    for k in range(KINDS):
        hi, lo = split(op_v[k])
        opf_v[k * PROFILE : (k + 1) * PROFILE, :] = jnp.concatenate([hi, lo], 1)
        hi, lo = split(jnp.transpose(op_v[k]))
        opb_v[k * PROFILE : (k + 1) * PROFILE, :] = jnp.concatenate([hi, lo], 1)

    def spread_profile(table, ct):
        return jnp.transpose(
            jnp.concatenate(
                [jnp.broadcast_to(table[ct * FIELDS + f : ct * FIELDS + f + 1, :], (PROFILE // FIELDS, LANES)) for f in range(FIELDS)], 0
            )
        )

    def ghosts(x, r):
        for j in range(HALO):
            x[r, j] = pltpu.roll(x[r, end - HALO + j], 1, 0)
            x[r, end + j] = pltpu.roll(x[r, first + j], 7, 0)

    def coefficients(r):
        table = rows_c[r]
        for ct, root in enumerate((root_a, root_b)):
            turn_v[ct] = spread_profile(table, ct)
            for i in range(SPAN):
                root[r, HALO + i] = turn_v[ct, pl.ds(i, 8, stride=SPAN), :]
            ghosts(root, r)

    def products(r, places):
        for i in places:
            a, b = root_a[r, i], root_b[r, i]
            mid_c[r, i] = 1.0 - 2.0 * (a * a + b * b)
            if i < WIDE - 1:
                lon_c[r, i] = a * root_a[r, i + 1]

    def products_lat(r, places):
        for i in places:
            lat_c[r, i] = root_b[r, i] * root_b[r + 1, i]

    @pl.loop(HALO, HALO + ROWS)
    def _(r):
        coefficients(r)
        ghosts(xa, r)

    all_but_one(codes_in, a2a_recv.at[0])
    codes_in[lat] = code_v[lat // per_tile]
    mod = lax.rem(lat, per_tile)
    lane_1 = lane_iota((1, LANES))
    for q in range(n_tiles):
        row = jnp.zeros((1, LANES), jnp.int32)
        for j in range(per_tile):
            moved = pltpu.roll(codes_in[q * per_tile + j], lax.rem(LANES + slots * (j - mod), LANES), 1)
            row = jnp.where(lane_1 // slots == j, moved, row)
        cell = (row - 1) >> 2
        cell = jnp.where(row > 0, (cell & -LANES) + (cell & (SPAN - 1)) * 8 + ((cell & (LANES - 1)) >> 4), -1)
        turned = jnp.transpose(jnp.broadcast_to(row.astype(F32), (LANES, LANES))).astype(jnp.int32)
        codet_v[q * LANES : (q + 1) * LANES, :] = turned
        across = jnp.transpose(jnp.broadcast_to(cell.astype(F32), (LANES, LANES))).astype(jnp.int32)
        down = jnp.broadcast_to(cell, (LANES, LANES))
        for r in range(ROWS):
            at = r * LANES
            oh_v[q * LANES : (q + 1) * LANES, at : at + LANES] = jnp.where(across == lane_iota((LANES, LANES)) + at, 1.0, 0.0).astype(BF16)
            oht_v[at : at + LANES, q * LANES : (q + 1) * LANES] = jnp.where(down == row_iota((LANES, LANES)) + at, 1.0, 0.0).astype(BF16)

    halo_rows = (0, 1, 2, 3, 12, 13, 14, 15)
    swaps = ((0, 3), (1, 2))
    for side in range(2):
        arrive(rows_c.at[pl.ds(3 * HALO * side, HALO)], recv_coef.at[side])
    for pole, base in ((south, 0), (north, 3 * HALO)):
        @pl.when(pole)
        def _():
            for p, q in swaps:
                one, two = rows_c[base + p], rows_c[base + q]
                rows_c[base + p] = two
                rows_c[base + q] = one

    @pl.loop(0, HALO)
    def _(r):
        coefficients(r)
        coefficients(r + 3 * HALO)

    @pl.loop(0, EXT)
    def _(r):
        products(r, range(HALO, HALO + SPAN))

    @pl.loop(0, EXT - 1)
    def _(r):
        products_lat(r, range(HALO, HALO + SPAN))

    arrive(tiles_in, recv_tile)
    side_tile = jnp.zeros((8, LANES), F32)
    for i in range(2):
        in_side = (lane >> 6) == i
        for e in range(EXT):
            if e < HALO:
                table, r = tiles_in[0, i], HALO + e - (1 + 2 * e) * south_i
            elif e < HALO + ROWS:
                table, r = tiles_in[2, i], e - HALO
            else:
                j = e - HALO - ROWS
                table, r = tiles_in[1, i], j + (ROWS - 1 - 2 * j) * north_i
            if HALO <= e < HALO + ROWS and e > HALO:
                continue
            if e == HALO:
                hit = in_side & ((lane & 63) >= 4 * HALO) & ((lane & 63) < 4 * (HALO + ROWS))
                side_tile = jnp.where(hit, pltpu.roll(table, 4 * HALO, 1), side_tile)
            else:
                moved = pltpu.roll(table, lax.rem(4 * (e - r) + LANES, LANES), 1)
                side_tile = jnp.where(in_side & ((lane & 63) >> 2 == e), moved, side_tile)
    for ct, root in enumerate((root_a, root_b)):
        turn_v[2 + ct] = spread_profile(side_tile, ct)
        for e in range(EXT):
            for j in range(HALO):
                root[e, j, 0:1, :] = turn_v[2 + ct, e * HALO + j : e * HALO + j + 1, :]
                root[e, end + j, 7:8, :] = turn_v[2 + ct, 64 + e * HALO + j : 65 + e * HALO + j, :]
    edge_places = (*range(HALO), *range(end, WIDE))

    @pl.loop(0, EXT)
    def _(r):
        products(r, (*edge_places, end - 1))

    @pl.loop(0, EXT - 1)
    def _(r):
        products_lat(r, edge_places)

    sign_south = jnp.where((lane >= LANES // 2) & south, -1.0, 1.0).astype(F32)
    sign_north = jnp.where((lane >= LANES // 2) & north, -1.0, 1.0).astype(F32)

    def complete(phase, x):
        for side, (pole, sign) in enumerate(((south, sign_south), (north, sign_north))):
            base = 3 * HALO * side
            arrive(x.at[pl.ds(base, HALO), inner], recv_row.at[phase, side])

            @pl.when(pole)
            def _():
                @pl.loop(first, end)
                def _(i):
                    for p, q in swaps:
                        one, two = x[base + p, i], x[base + q, i]
                        x[base + p, i] = two * sign
                        x[base + q, i] = one * sign

        @pl.loop(0, HALO)
        def _(r):
            ghosts(x, r)
            ghosts(x, r + 3 * HALO)

        arrive(from_side.at[phase], recv_side.at[phase])
        arrive(from_corner.at[phase], recv_corner.at[phase])
        for r in range(ROWS):
            for j in range(HALO):
                at = r % 2 * HALO + j
                x[r + HALO, j, 0:1, :] = from_side[phase, 0, r // 2, at : at + 1, :]
                x[r + HALO, end + j, 7:8, :] = from_side[phase, 1, r // 2, at : at + 1, :]
        for side, sign in enumerate((sign_south, sign_north)):
            west, east = from_corner[phase, side, 0] * sign, from_corner[phase, side, 1] * sign
            for k, at, n in CORNER:
                r = HALO - k if side == 0 else HALO + ROWS - 1 + k
                for j in range(n):
                    x[r, HALO - n + j, 0:1, :] = west[at + j : at + j + 1, :]
                    x[r, end + j, 7:8, :] = east[at + j : at + j + 1, :]

    def diffuse(x):
        for t, (src, dst) in enumerate(((x, ya), (ya, za), (za, ya), (ya, za))):
            @pl.loop(t + 1, EXT - 1 - t)
            def _(r):
                f = {i: src[r, i] for i in range(t, WIDE - t)}
                for i in range(t + 1, WIDE - 1 - t):
                    dst[r, i] = (
                        mid_c[r, i] * f[i]
                        + (lon_c[r, i - 1] * f[i - 1] + lon_c[r, i] * f[i + 1])
                        + (lat_c[r - 1, i] * src[r - 1, i] + lat_c[r, i] * src[r + 1, i])
                    )

    complete(0, xa)
    diffuse(xa)

    @pl.loop(0, ROWS)
    def _(r):
        v = za[r + HALO, first:end].reshape(LANES, PROFILE)
        hi, lo = split(v)
        st_v[pl.ds(pl.multiple_of(r * LANES, LANES), LANES), :] = jnp.concatenate([hi, lo], 1)

    found = jnp.dot(oh_v[...], st_v[...], preferred_element_type=F32)
    columns = found[:, :PROFILE] + found[:, PROFILE:]

    def by_kind(values, table):
        hi, lo = split(values)
        kind = (codet_v[...] - 1) & 3
        for k in range(KINDS):
            of_kind = kind == k
            lhs_hi[:, k * PROFILE : (k + 1) * PROFILE] = jnp.where(of_kind, hi.astype(F32), 0.0).astype(BF16)
            lhs_lo[:, k * PROFILE : (k + 1) * PROFILE] = jnp.where(of_kind, lo.astype(F32), 0.0).astype(BF16)
        one = jnp.dot(lhs_hi[...], table[...], preferred_element_type=F32)
        two = jnp.dot(lhs_lo[...], table[:, :PROFILE], preferred_element_type=F32)
        return one[:, :PROFILE] + one[:, PROFILE:] + two

    model = by_kind(columns, opf_v)
    for copy in own:
        copy.wait()
    all_but_one(obs_v, a2a_recv.at[1])
    all_but_one(wgt_v, a2a_recv.at[2])
    dep = jnp.where(codet_v[...] > 0, obs_v[...] - model, 0.0)
    dep_v[...] = dep
    adj = by_kind(wgt_v[...] * dep, opb_v)
    hi, lo = split(adj)
    adj_v[...] = jnp.concatenate([hi, lo], 1)
    forcing = jnp.dot(oht_v[...], adj_v[...], preferred_element_type=F32)
    forcing = forcing[:, :PROFILE] + forcing[:, PROFILE:]
    for r in range(ROWS):
        xe[r + HALO, first:end] = forcing[r * LANES : (r + 1) * LANES].reshape(SPAN, 8, PROFILE)
    stage(1, xe)
    sent += start(small_copies(1) + row_copies(1, xe))

    back = pltpu.make_async_copy(dep_v.at[mine], dep_o.at[mine], own_sem.at[2])
    back.start()

    @pl.loop(1, n_lat)
    def _(k):
        to = lax.rem(lat + k, n_lat)
        theirs = pl.ds(pl.multiple_of(to * slots, slots), slots)
        pltpu.make_async_remote_copy(
            src_ref=dep_v.at[theirs], dst_ref=dep_o.at[mine], send_sem=a2a_send.at[3], recv_sem=a2a_recv.at[3],
            device_id=dev((lon, to)), device_id_type=pl.DeviceIdType.MESH,
        ).start()

    @pl.loop(HALO, HALO + ROWS)
    def _(r):
        ghosts(xe, r)

    complete(1, xe)
    diffuse(xe)

    @pl.loop(0, ROWS)
    def _(r):
        for i in range(SPAN):
            turn_v[r, pl.ds(i, 8, stride=SPAN), :] = za[r + HALO, HALO + i]
        rows = pl.ds(r, PROFILE, stride=ROWS)
        grad_o[rows, :] = inc_v[rows, :] - jnp.transpose(turn_v[r])

    for copy in sent:
        copy.wait_send()
    all_but_one(codes_in, a2a_send.at[0])
    all_but_one(obs_v, a2a_send.at[1])
    all_but_one(wgt_v, a2a_send.at[2])
    all_but_one(dep_v, a2a_send.at[3])
    all_but_one(dep_o, a2a_recv.at[3])
    back.wait()


def local(n_lon, n_lat, increment, coef_lon, coef_lat, obs_values, obs_weight, obs_operator, obs_columns, obs_types, obs_counts):
    n_rows = obs_columns.shape[0]
    slots = n_rows // n_lat
    tiles = n_rows // LANES
    cells = ROWS * LANES
    vmem = pl.BlockSpec(memory_space=pltpu.VMEM)
    block = pltpu.VMEM((EXT, WIDE, 8, PROFILE), F32)
    gradient, departures = pl.pallas_call(
        functools.partial(kernel, n_lon, n_lat, slots),
        out_shape=(
            jax.ShapeDtypeStruct((PROFILE * ROWS, LANES), F32),
            jax.ShapeDtypeStruct((n_rows, PROFILE), F32),
        ),
        in_specs=[pl.BlockSpec(memory_space=pltpu.HBM)] * 9,
        out_specs=(vmem, vmem),
        scratch_shapes=[
            pltpu.VMEM((PROFILE * ROWS, LANES), F32),
            pltpu.VMEM((2, FIELDS * ROWS, LANES), F32),
            pltpu.VMEM((KINDS, PROFILE, PROFILE), F32),
            pltpu.VMEM((tiles, LANES), jnp.int32),
            pltpu.VMEM((tiles, LANES), jnp.int32),
            pltpu.VMEM((1, n_lat), jnp.int32),
            pltpu.VMEM((n_rows, PROFILE), F32),
            pltpu.VMEM((n_rows, PROFILE), F32),
            pltpu.VMEM((tiles, 1, LANES), jnp.int32),
            pltpu.VMEM((n_lat, 1, LANES), jnp.int32),
            pltpu.VMEM((n_rows, LANES), jnp.int32),
            pltpu.VMEM((n_rows, PROFILE), F32),
            block, block, block, block,
            pltpu.VMEM((ROWS, LANES, PROFILE), F32),
            pltpu.VMEM((EXT, 8, LANES), F32),
            pltpu.VMEM((1, 8, LANES), F32),
            pltpu.VMEM((3, 2, 8, LANES), F32),
            pltpu.VMEM((2, 2, 4, 8, PROFILE), F32),
            pltpu.VMEM((2, 2, 2, 8, PROFILE), F32),
            pltpu.VMEM((2, 2, 4, 8, PROFILE), F32),
            pltpu.VMEM((2, 2, 2, 8, PROFILE), F32),
            pltpu.VMEM((7, 8, PROFILE), F32),
            block, block, block, block, block,
            pltpu.VMEM((cells, 2 * PROFILE), BF16),
            pltpu.VMEM((n_rows, cells), BF16),
            pltpu.VMEM((cells, n_rows), BF16),
            pltpu.VMEM((KINDS * PROFILE, 2 * PROFILE), BF16),
            pltpu.VMEM((KINDS * PROFILE, 2 * PROFILE), BF16),
            pltpu.VMEM((n_rows, KINDS * PROFILE), BF16),
            pltpu.VMEM((n_rows, KINDS * PROFILE), BF16),
            pltpu.VMEM((n_rows, 2 * PROFILE), BF16),
            pltpu.SemaphoreType.DMA((7,)),
            pltpu.SemaphoreType.DMA((3,)),
            pltpu.SemaphoreType.DMA((2, 2)),
            pltpu.SemaphoreType.DMA((2, 2, 2)),
            pltpu.SemaphoreType.DMA((3, 2)),
            pltpu.SemaphoreType.DMA((3, 2)),
            pltpu.SemaphoreType.DMA((2,)),
            pltpu.SemaphoreType.DMA((2,)),
            pltpu.SemaphoreType.DMA,
            pltpu.SemaphoreType.DMA((2, 2)),
            pltpu.SemaphoreType.DMA((2,)),
            pltpu.SemaphoreType.DMA((6,)),
            pltpu.SemaphoreType.DMA((4,)),
            pltpu.SemaphoreType.DMA((4,)),
            pltpu.SemaphoreType.DMA((4,)),
        ],
        compiler_params=pltpu.CompilerParams(collective_id=0, has_side_effects=True, vmem_limit_bytes=56 * 1024 * 1024),
        name="assimilate",
    )(*(
        pltpu.with_memory_space_constraint(x, pltpu.HBM)
        for x in (
            increment.reshape(PROFILE * ROWS, LANES),
            coef_lon.reshape(FIELDS * ROWS, LANES),
            coef_lat.reshape(FIELDS * ROWS, LANES),
            obs_values,
            obs_weight,
            obs_operator,
            obs_columns.reshape(tiles, LANES),
            obs_types.reshape(tiles, LANES),
            obs_counts.reshape(1, n_lat),
        )
    ))
    return gradient.reshape(increment.shape), departures


def solution(mesh):
    return jax.shard_map(
        functools.partial(local, mesh.shape["lon"], mesh.shape["lat"]),
        mesh=mesh,
        in_specs=(
            P(None, None, "lat", "lon"),
            P(None, "lat", "lon"),
            P(None, "lat", "lon"),
            P(("lon", "lat"), None),
            P(("lon", "lat"), None),
            P(),
            P(("lon", "lat")),
            P(("lon", "lat")),
            P(("lon", "lat")),
        ),
        out_specs=(P(None, None, "lat", "lon"), P(("lon", "lat"), None)),
        check_vma=False,
    )
```

```python
import functools

import jax
import jax.numpy as jnp
from jax import lax
from jax.experimental import pallas as pl
from jax.experimental.pallas import tpu as pltpu
from jax.sharding import PartitionSpec as P

HALO = 4
STEPS = 4
ROWS = 8
EXT = ROWS + 2 * HALO
LANES = 128
SPAN = LANES // 8
WIDE = SPAN + 2 * HALO
FIELDS = 4
PROFILE = 128
KINDS = 3
F32 = jnp.float32
BF16 = jnp.bfloat16
CORNER = ((1, 0, 3), (2, 3, 2), (3, 5, 1))


def lane_iota(shape):
    return lax.broadcasted_iota(jnp.int32, shape, len(shape) - 1)


def row_iota(shape):
    return lax.broadcasted_iota(jnp.int32, shape, 0)


def split(x):
    hi = x.astype(BF16)
    return hi, (x - hi.astype(F32)).astype(BF16)


def kernel(
    n_lon, n_lat, slots,
    inc_h, clon_h, clat_h, obs_h, wgt_h, op_h, col_h, typ_h, cnt_h,
    grad_o, dep_o,
    inc_v, cf_v, op_v, col_v, typ_v, cnt_v, obs_v, wgt_v, code_v, codes_in, codet_v, dep_v,
    xa, xe, ya, za, turn_v, rows_c, tile_v, tiles_in, side_v, corner_v, from_side, from_corner, relay_v,
    root_a, root_b, mid_c, lon_c, lat_c, st_v, oh_v, oht_v, opf_v, opb_v, lhs_hi, lhs_lo, adj_v,
    load_sem, own_sem, side_send, corner_send, tile_send, row_send, recv_side, recv_corner, recv_tile, recv_row, recv_coef,
    relay_send, relay_recv, a2a_send, a2a_recv, ready_sem,
):
    lon, lat = lax.axis_index("lon"), lax.axis_index("lat")
    n_rows = n_lat * slots
    n_tiles = n_rows // LANES
    per_tile = LANES // slots
    south, north = lat == 0, lat == n_lat - 1
    south_i, north_i = south.astype(jnp.int32), north.astype(jnp.int32)
    opposite = n_lon // 2

    def lon_at(by):
        return lax.rem(lon + by + n_lon, n_lon)

    def prev_of(d):
        return (lon_at(d + opposite * south_i), lat - 1 + south_i)

    def next_of(d):
        return (lon_at(d + opposite * north_i), lat + 1 - north_i)

    last, after = lax.rem(lon, opposite) == opposite - 1, lax.rem(lon, opposite) == 0
    last_i, after_i = last.astype(jnp.int32), after.astype(jnp.int32)

    def dev(where):
        return {"lon": where[0], "lat": where[1]}

    barrier = pltpu.get_barrier_semaphore()

    def greet(where):
        pl.semaphore_signal(barrier, inc=1, device_id=dev(where), device_id_type=pl.DeviceIdType.MESH)

    for where in (prev_of(-1), next_of(-1), (lon_at(-1), lat)):
        greet(where)

    @pl.when(south)
    def _():
        greet(prev_of(0))

    @pl.when(north)
    def _():
        greet(next_of(0))

    @pl.when(last)
    def _():
        greet((lon_at(opposite), lat))

    @pl.when(after)
    def _():
        greet((lon_at(opposite), lat))
        greet((lon_at(opposite - 1), lat))

    @pl.when(after & ~south)
    def _():
        greet((lon_at(opposite - 1), lat - 1))

    @pl.when(after & ~north)
    def _():
        greet((lon_at(opposite - 1), lat + 1))

    @pl.loop(1, n_lat)
    def _(k):
        greet((lon, lax.rem(lat + k, n_lat)))

    loads = [
        pltpu.make_async_copy(src, dst, load_sem.at[i])
        for i, (src, dst) in enumerate(
            (
                (inc_h, inc_v), (clon_h, cf_v.at[0]), (clat_h, cf_v.at[1]), (op_h, op_v),
                (col_h, col_v), (typ_h, typ_v), (cnt_h, cnt_v),
            )
        )
    ]
    for load in loads:
        load.start()
    mine = pl.ds(pl.multiple_of(lat * slots, slots), slots)
    own = [
        pltpu.make_async_copy(obs_h.at[mine], obs_v.at[mine], own_sem.at[0]),
        pltpu.make_async_copy(wgt_h.at[mine], wgt_v.at[mine], own_sem.at[1]),
    ]
    for copy in own:
        copy.start()

    for i in (4, 5, 6):
        loads[i].wait()
    rep = (lane_iota((n_lat, n_rows)) // slots == row_iota((n_lat, n_rows))).astype(F32).astype(BF16)
    counts = jnp.broadcast_to(cnt_v[...].astype(F32), (8, n_lat)).astype(BF16)
    limit = jnp.dot(counts, rep, preferred_element_type=F32)
    for q in range(n_tiles):
        lim = limit[0:1, q * LANES : (q + 1) * LANES].astype(jnp.int32)
        code = col_v[q : q + 1, :] * 4 + typ_v[q : q + 1, :] + 1
        code_v[q] = jnp.where(lane_iota((1, LANES)) % slots < lim, code, 0)

    for i in (0, 1, 2):
        loads[i].wait()

    @pl.loop(0, ROWS)
    def _(r):
        turn_v[r] = jnp.transpose(inc_v[pl.ds(r, PROFILE, stride=ROWS), :])
        for i in range(SPAN):
            xa[r + HALO, HALO + i] = turn_v[r, pl.ds(i, 8, stride=SPAN), :]
        for ct in range(2):
            rows_c[r + HALO, ct * FIELDS : (ct + 1) * FIELDS, :] = cf_v[ct, pl.ds(r, FIELDS, stride=ROWS), :]

    first, end = HALO, HALO + SPAN

    def stage(phase, x):
        for r in range(ROWS):
            for j in range(HALO):
                at = r % 2 * HALO + j
                side_v[phase, 0, r // 2, at : at + 1, :] = x[r + HALO, end - HALO + j, 7:8, :]
                side_v[phase, 1, r // 2, at : at + 1, :] = x[r + HALO, first + j, 0:1, :]
        for half in range(2):
            for k, at, n in CORNER:
                r = HALO + k - 1 if half == 0 else HALO + ROWS - k
                for j in range(n):
                    corner_v[phase, half, 0, at + j : at + j + 1, :] = x[r, end - n + j, 7:8, :]
                    corner_v[phase, half, 1, at + j : at + j + 1, :] = x[r, first + j, 0:1, :]

    stage(0, xa)
    lane = lane_iota((8, LANES))
    tile = jnp.zeros((8, LANES), F32)
    for r in range(ROWS):
        v = rows_c[r + HALO]
        tile = jnp.where(lane >> 2 == r, pltpu.roll(v, 4 * r + HALO, 1), tile)
        tile = jnp.where(lane >> 2 == r + 16, pltpu.roll(v, 64 + 4 * r, 1), tile)
    tile_v[0] = tile

    pl.semaphore_wait(barrier, n_lat - 1 + 3 + south_i + north_i + last_i * (4 - south_i - north_i) + after_i)

    for by, row in ((1, lat), (1 + opposite * south_i, lat - 1 + south_i), (1 + opposite * north_i, lat + 1 - north_i)):
        by = jnp.where(last, 1 - opposite, by)
        pl.semaphore_signal(ready_sem, inc=1, device_id=dev((lon_at(by), row)), device_id_type=pl.DeviceIdType.MESH)

    low, high = pl.ds(HALO, HALO), pl.ds(2 * HALO, HALO)
    inner = pl.ds(HALO, SPAN)
    to_prev = pl.ds(3 * HALO * (1 - south_i), HALO)
    to_next = pl.ds(3 * HALO * north_i, HALO)
    prev_side, next_side = 1 - south_i, north_i

    def send(src, dst, send_at, sem, where):
        return pltpu.make_async_remote_copy(
            src_ref=src, dst_ref=dst, send_sem=send_at, recv_sem=sem,
            device_id=dev(where), device_id_type=pl.DeviceIdType.MESH,
        )

    def start(copies):
        for copy in copies:
            copy.start()
        return copies

    class Routed:
        def __init__(self, other, plain, changed):
            self.other, self.plain, self.changed = other, plain, changed

        def ahead(self):
            pl.when(self.other)(self.changed.start)

        def start(self):
            pl.when(~self.other)(self.plain.start)

        def wait_send(self):
            self.plain.wait_send()

    class Only:
        def __init__(self, holds, copy):
            self.holds, self.copy = holds, copy

        def ahead(self):
            pass

        def start(self):
            pl.when(self.holds)(self.copy.start)

        def wait_send(self):
            pl.when(self.holds)(self.copy.wait_send)

    ends = (last, after)

    def by_relay(i, part, src, send_at):
        at = relay_v.at[i, pl.ds(*((0, 4), (4, 1), (5, 1), (6, 1))[part])]
        return send(src, at, send_at, relay_recv.at[i, part], (lon_at(opposite), lat))

    def small_copies(phase, *to):
        copies = []
        for i in to:
            d = 1 - 2 * i
            src, send_at = side_v.at[phase, i], side_send.at[phase, i]
            copy = send(src, from_side.at[phase, i], send_at, recv_side.at[phase], (lon_at(d), lat))
            copies.append(copy if phase else Routed(ends[i], copy, by_relay(i, 0, src, send_at)))
            for half, side, where, pole in ((0, prev_side, prev_of(d), south), (1, next_side, next_of(d), north)):
                src, send_at = corner_v.at[phase, half, pl.ds(i, 1)], corner_send.at[phase, half, i]
                copy = send(src, from_corner.at[phase, side, pl.ds(i, 1)], send_at, recv_corner.at[phase], where)
                copies.append(copy if phase else Routed(ends[i] & ~pole, copy, by_relay(i, 1 + half, src, send_at)))
        return copies

    def tile_copies(*to):
        copies = []
        for i in to:
            d = 1 - 2 * i
            for v, (at, where, pole) in enumerate(
                ((2, (lon_at(d), lat), None), (prev_side, prev_of(d), south), (next_side, next_of(d), north))
            ):
                copy = send(tile_v, tiles_in.at[at, pl.ds(i, 1)], tile_send.at[v, i], recv_tile, where)
                if v == 0:
                    copies.append(Routed(ends[i], copy, by_relay(i, 3, tile_v, tile_send.at[v, i])))
                else:
                    copies.append(Only(~ends[i] | pole, copy))
        return copies

    def pass_on(i):
        over, end_of = lon_at((1 - opposite) * (1 - 2 * i)), ends[i]
        ways = [
            (end_of, 0, (0, 4), from_side.at[0, i], recv_side.at[0], lat),
            (end_of & ~south, 1, (4, 1), from_corner.at[0, 1, pl.ds(i, 1)], recv_corner.at[0], lat - 1),
            (end_of & ~north, 2, (5, 1), from_corner.at[0, 0, pl.ds(i, 1)], recv_corner.at[0], lat + 1),
            (end_of, 3, (6, 1), tiles_in.at[2, pl.ds(i, 1)], recv_tile, lat),
            (end_of & ~south, None, (6, 1), tiles_in.at[1, pl.ds(i, 1)], recv_tile, lat - 1),
            (end_of & ~north, None, (6, 1), tiles_in.at[0, pl.ds(i, 1)], recv_tile, lat + 1),
        ]
        copies = []
        for n, (holds, part, (at, count), dst, sem, to) in enumerate(ways):
            src = relay_v.at[i, pl.ds(at, count)]
            copy = Only(holds, send(src, dst, relay_send.at[i, n], sem, (over, to)))
            if part is not None:
                arrived = pltpu.make_async_copy(src, src, relay_recv.at[i, part])
                pl.when(holds)(arrived.wait)
            copy.start()
            copies.append(copy)
        return copies

    def row_copies(phase, x):
        return [
            send(x.at[low, inner], x.at[to_prev, inner], row_send.at[phase, 0], recv_row.at[phase, prev_side], prev_of(0)),
            send(x.at[high, inner], x.at[to_next, inner], row_send.at[phase, 1], recv_row.at[phase, next_side], next_of(0)),
        ]

    def coef_copies():
        return [
            send(rows_c.at[low], rows_c.at[to_prev], row_send.at[2, 0], recv_coef.at[prev_side], prev_of(0)),
            send(rows_c.at[high], rows_c.at[to_next], row_send.at[2, 1], recv_coef.at[next_side], next_of(0)),
        ]

    def arrive(ref, sem):
        pltpu.make_async_copy(ref, ref, sem).wait()

    eastward, westward = small_copies(0, 0) + tile_copies(0), small_copies(0, 1) + tile_copies(1)
    for copy in eastward + westward:
        copy.ahead()
    sent = start(eastward + coef_copies())

    @pl.loop(1, n_lat)
    def _(k):
        to = lax.rem(lat + k, n_lat)
        pltpu.make_async_remote_copy(
            src_ref=code_v.at[to // per_tile], dst_ref=codes_in.at[lat], send_sem=a2a_send.at[0], recv_sem=a2a_recv.at[0],
            device_id=dev((lon, to)), device_id_type=pl.DeviceIdType.MESH,
        ).start()

    sent += start(row_copies(0, xa))

    @pl.loop(1, n_lat)
    def _(k):
        to = lax.rem(lat + k, n_lat)
        theirs = pl.ds(pl.multiple_of(to * slots, slots), slots)
        for i, (src, dst) in enumerate(((obs_h, obs_v), (wgt_h, wgt_v))):
            pltpu.make_async_remote_copy(
                src_ref=src.at[theirs], dst_ref=dst.at[mine], send_sem=a2a_send.at[1 + i], recv_sem=a2a_recv.at[1 + i],
                device_id=dev((lon, to)), device_id_type=pl.DeviceIdType.MESH,
            ).start()

    def all_but_one(ref, sem):
        part = ref.at[pl.ds(0, ref.shape[0] // n_lat * (n_lat - 1))]
        pltpu.make_async_copy(part, part, sem).wait()

    loads[3].wait()
    for k in range(KINDS):
        hi, lo = split(op_v[k])
        opf_v[k * PROFILE : (k + 1) * PROFILE, :] = jnp.concatenate([hi, lo], 1)
        hi, lo = split(jnp.transpose(op_v[k]))
        opb_v[k * PROFILE : (k + 1) * PROFILE, :] = jnp.concatenate([hi, lo], 1)

    def spread_profile(table, ct):
        return jnp.transpose(
            jnp.concatenate(
                [jnp.broadcast_to(table[ct * FIELDS + f : ct * FIELDS + f + 1, :], (PROFILE // FIELDS, LANES)) for f in range(FIELDS)], 0
            )
        )

    def ghosts(x, r):
        for j in range(HALO):
            x[r, j] = pltpu.roll(x[r, end - HALO + j], 1, 0)
            x[r, end + j] = pltpu.roll(x[r, first + j], 7, 0)

    def coefficients(r):
        table = rows_c[r]
        for ct, root in enumerate((root_a, root_b)):
            turn_v[ct] = spread_profile(table, ct)
            for i in range(SPAN):
                root[r, HALO + i] = turn_v[ct, pl.ds(i, 8, stride=SPAN), :]
            ghosts(root, r)

    def products(r, places):
        for i in places:
            a, b = root_a[r, i], root_b[r, i]
            mid_c[r, i] = 1.0 - 2.0 * (a * a + b * b)
            if i < WIDE - 1:
                lon_c[r, i] = a * root_a[r, i + 1]

    def products_lat(r, places):
        for i in places:
            lat_c[r, i] = root_b[r, i] * root_b[r + 1, i]

    @pl.loop(HALO, HALO + ROWS)
    def _(r):
        coefficients(r)
        ghosts(xa, r)

    sent += pass_on(0)
    all_but_one(codes_in, a2a_recv.at[0])
    codes_in[lat] = code_v[lat // per_tile]
    mod = lax.rem(lat, per_tile)
    lane_1 = lane_iota((1, LANES))
    for q in range(n_tiles):
        row = jnp.zeros((1, LANES), jnp.int32)
        for j in range(per_tile):
            moved = pltpu.roll(codes_in[q * per_tile + j], lax.rem(LANES + slots * (j - mod), LANES), 1)
            row = jnp.where(lane_1 // slots == j, moved, row)
        cell = (row - 1) >> 2
        cell = jnp.where(row > 0, (cell & -LANES) + (cell & (SPAN - 1)) * 8 + ((cell & (LANES - 1)) >> 4), -1)
        turned = jnp.transpose(jnp.broadcast_to(row.astype(F32), (LANES, LANES))).astype(jnp.int32)
        codet_v[q * LANES : (q + 1) * LANES, :] = turned
        across = jnp.transpose(jnp.broadcast_to(cell.astype(F32), (LANES, LANES))).astype(jnp.int32)
        down = jnp.broadcast_to(cell, (LANES, LANES))
        for r in range(ROWS):
            at = r * LANES
            oh_v[q * LANES : (q + 1) * LANES, at : at + LANES] = jnp.where(across == lane_iota((LANES, LANES)) + at, 1.0, 0.0).astype(BF16)
            oht_v[at : at + LANES, q * LANES : (q + 1) * LANES] = jnp.where(down == row_iota((LANES, LANES)) + at, 1.0, 0.0).astype(BF16)

    halo_rows = (0, 1, 2, 3, 12, 13, 14, 15)
    swaps = ((0, 3), (1, 2))
    for side in range(2):
        arrive(rows_c.at[pl.ds(3 * HALO * side, HALO)], recv_coef.at[side])
    for pole, base in ((south, 0), (north, 3 * HALO)):
        @pl.when(pole)
        def _():
            for p, q in swaps:
                one, two = rows_c[base + p], rows_c[base + q]
                rows_c[base + p] = two
                rows_c[base + q] = one

    @pl.loop(0, HALO)
    def _(r):
        coefficients(r)
        coefficients(r + 3 * HALO)

    @pl.loop(0, EXT)
    def _(r):
        products(r, range(HALO, HALO + SPAN))

    @pl.loop(0, EXT - 1)
    def _(r):
        products_lat(r, range(HALO, HALO + SPAN))

    pl.semaphore_wait(ready_sem, 3)
    sent += start(westward) + pass_on(1)

    arrive(tiles_in, recv_tile)
    side_tile = jnp.zeros((8, LANES), F32)
    for i in range(2):
        in_side = (lane >> 6) == i
        for e in range(EXT):
            if e < HALO:
                table, r = tiles_in[0, i], HALO + e - (1 + 2 * e) * south_i
            elif e < HALO + ROWS:
                table, r = tiles_in[2, i], e - HALO
            else:
                j = e - HALO - ROWS
                table, r = tiles_in[1, i], j + (ROWS - 1 - 2 * j) * north_i
            if HALO <= e < HALO + ROWS and e > HALO:
                continue
            if e == HALO:
                hit = in_side & ((lane & 63) >= 4 * HALO) & ((lane & 63) < 4 * (HALO + ROWS))
                side_tile = jnp.where(hit, pltpu.roll(table, 4 * HALO, 1), side_tile)
            else:
                moved = pltpu.roll(table, lax.rem(4 * (e - r) + LANES, LANES), 1)
                side_tile = jnp.where(in_side & ((lane & 63) >> 2 == e), moved, side_tile)
    for ct, root in enumerate((root_a, root_b)):
        turn_v[2 + ct] = spread_profile(side_tile, ct)
        for e in range(EXT):
            for j in range(HALO):
                root[e, j, 0:1, :] = turn_v[2 + ct, e * HALO + j : e * HALO + j + 1, :]
                root[e, end + j, 7:8, :] = turn_v[2 + ct, 64 + e * HALO + j : 65 + e * HALO + j, :]
    edge_places = (*range(HALO), *range(end, WIDE))

    @pl.loop(0, EXT)
    def _(r):
        products(r, (*edge_places, end - 1))

    @pl.loop(0, EXT - 1)
    def _(r):
        products_lat(r, edge_places)

    sign_south = jnp.where((lane >= LANES // 2) & south, -1.0, 1.0).astype(F32)
    sign_north = jnp.where((lane >= LANES // 2) & north, -1.0, 1.0).astype(F32)

    def complete(phase, x):
        for side, (pole, sign) in enumerate(((south, sign_south), (north, sign_north))):
            base = 3 * HALO * side
            arrive(x.at[pl.ds(base, HALO), inner], recv_row.at[phase, side])

            @pl.when(pole)
            def _():
                @pl.loop(first, end)
                def _(i):
                    for p, q in swaps:
                        one, two = x[base + p, i], x[base + q, i]
                        x[base + p, i] = two * sign
                        x[base + q, i] = one * sign

        @pl.loop(0, HALO)
        def _(r):
            ghosts(x, r)
            ghosts(x, r + 3 * HALO)

        arrive(from_side.at[phase], recv_side.at[phase])
        arrive(from_corner.at[phase], recv_corner.at[phase])
        for r in range(ROWS):
            for j in range(HALO):
                at = r % 2 * HALO + j
                x[r + HALO, j, 0:1, :] = from_side[phase, 0, r // 2, at : at + 1, :]
                x[r + HALO, end + j, 7:8, :] = from_side[phase, 1, r // 2, at : at + 1, :]
        for side, sign in enumerate((sign_south, sign_north)):
            west, east = from_corner[phase, side, 0] * sign, from_corner[phase, side, 1] * sign
            for k, at, n in CORNER:
                r = HALO - k if side == 0 else HALO + ROWS - 1 + k
                for j in range(n):
                    x[r, HALO - n + j, 0:1, :] = west[at + j : at + j + 1, :]
                    x[r, end + j, 7:8, :] = east[at + j : at + j + 1, :]

    def diffuse(x):
        for t, (src, dst) in enumerate(((x, ya), (ya, za), (za, ya), (ya, za))):
            @pl.loop(t + 1, EXT - 1 - t)
            def _(r):
                f = {i: src[r, i] for i in range(t, WIDE - t)}
                for i in range(t + 1, WIDE - 1 - t):
                    dst[r, i] = (
                        mid_c[r, i] * f[i]
                        + (lon_c[r, i - 1] * f[i - 1] + lon_c[r, i] * f[i + 1])
                        + (lat_c[r - 1, i] * src[r - 1, i] + lat_c[r, i] * src[r + 1, i])
                    )

    complete(0, xa)
    diffuse(xa)

    @pl.loop(0, ROWS)
    def _(r):
        v = za[r + HALO, first:end].reshape(LANES, PROFILE)
        hi, lo = split(v)
        st_v[pl.ds(pl.multiple_of(r * LANES, LANES), LANES), :] = jnp.concatenate([hi, lo], 1)

    found = jnp.dot(oh_v[...], st_v[...], preferred_element_type=F32)
    columns = found[:, :PROFILE] + found[:, PROFILE:]

    def by_kind(values, table):
        hi, lo = split(values)
        kind = (codet_v[...] - 1) & 3
        for k in range(KINDS):
            of_kind = kind == k
            lhs_hi[:, k * PROFILE : (k + 1) * PROFILE] = jnp.where(of_kind, hi.astype(F32), 0.0).astype(BF16)
            lhs_lo[:, k * PROFILE : (k + 1) * PROFILE] = jnp.where(of_kind, lo.astype(F32), 0.0).astype(BF16)
        one = jnp.dot(lhs_hi[...], table[...], preferred_element_type=F32)
        two = jnp.dot(lhs_lo[...], table[:, :PROFILE], preferred_element_type=F32)
        return one[:, :PROFILE] + one[:, PROFILE:] + two

    model = by_kind(columns, opf_v)
    for copy in own:
        copy.wait()
    all_but_one(obs_v, a2a_recv.at[1])
    all_but_one(wgt_v, a2a_recv.at[2])
    dep = jnp.where(codet_v[...] > 0, obs_v[...] - model, 0.0)
    dep_v[...] = dep
    adj = by_kind(wgt_v[...] * dep, opb_v)
    hi, lo = split(adj)
    adj_v[...] = jnp.concatenate([hi, lo], 1)
    forcing = jnp.dot(oht_v[...], adj_v[...], preferred_element_type=F32)
    forcing = forcing[:, :PROFILE] + forcing[:, PROFILE:]
    for r in range(ROWS):
        xe[r + HALO, first:end] = forcing[r * LANES : (r + 1) * LANES].reshape(SPAN, 8, PROFILE)
    stage(1, xe)
    sent += start(small_copies(1, 0, 1) + row_copies(1, xe))

    back = pltpu.make_async_copy(dep_v.at[mine], dep_o.at[mine], own_sem.at[2])
    back.start()

    @pl.loop(1, n_lat)
    def _(k):
        to = lax.rem(lat + k, n_lat)
        theirs = pl.ds(pl.multiple_of(to * slots, slots), slots)
        pltpu.make_async_remote_copy(
            src_ref=dep_v.at[theirs], dst_ref=dep_o.at[mine], send_sem=a2a_send.at[3], recv_sem=a2a_recv.at[3],
            device_id=dev((lon, to)), device_id_type=pl.DeviceIdType.MESH,
        ).start()

    @pl.loop(HALO, HALO + ROWS)
    def _(r):
        ghosts(xe, r)

    complete(1, xe)
    diffuse(xe)

    @pl.loop(0, ROWS)
    def _(r):
        for i in range(SPAN):
            turn_v[r, pl.ds(i, 8, stride=SPAN), :] = za[r + HALO, HALO + i]
        rows = pl.ds(r, PROFILE, stride=ROWS)
        grad_o[rows, :] = inc_v[rows, :] - jnp.transpose(turn_v[r])

    for copy in sent:
        copy.wait_send()
    all_but_one(codes_in, a2a_send.at[0])
    all_but_one(obs_v, a2a_send.at[1])
    all_but_one(wgt_v, a2a_send.at[2])
    all_but_one(dep_v, a2a_send.at[3])
    all_but_one(dep_o, a2a_recv.at[3])
    back.wait()


def local(n_lon, n_lat, increment, coef_lon, coef_lat, obs_values, obs_weight, obs_operator, obs_columns, obs_types, obs_counts):
    n_rows = obs_columns.shape[0]
    slots = n_rows // n_lat
    tiles = n_rows // LANES
    cells = ROWS * LANES
    vmem = pl.BlockSpec(memory_space=pltpu.VMEM)
    block = pltpu.VMEM((EXT, WIDE, 8, PROFILE), F32)
    gradient, departures = pl.pallas_call(
        functools.partial(kernel, n_lon, n_lat, slots),
        out_shape=(
            jax.ShapeDtypeStruct((PROFILE * ROWS, LANES), F32),
            jax.ShapeDtypeStruct((n_rows, PROFILE), F32),
        ),
        in_specs=[pl.BlockSpec(memory_space=pltpu.HBM)] * 9,
        out_specs=(vmem, vmem),
        scratch_shapes=[
            pltpu.VMEM((PROFILE * ROWS, LANES), F32),
            pltpu.VMEM((2, FIELDS * ROWS, LANES), F32),
            pltpu.VMEM((KINDS, PROFILE, PROFILE), F32),
            pltpu.VMEM((tiles, LANES), jnp.int32),
            pltpu.VMEM((tiles, LANES), jnp.int32),
            pltpu.VMEM((1, n_lat), jnp.int32),
            pltpu.VMEM((n_rows, PROFILE), F32),
            pltpu.VMEM((n_rows, PROFILE), F32),
            pltpu.VMEM((tiles, 1, LANES), jnp.int32),
            pltpu.VMEM((n_lat, 1, LANES), jnp.int32),
            pltpu.VMEM((n_rows, LANES), jnp.int32),
            pltpu.VMEM((n_rows, PROFILE), F32),
            block, block, block, block,
            pltpu.VMEM((ROWS, LANES, PROFILE), F32),
            pltpu.VMEM((EXT, 8, LANES), F32),
            pltpu.VMEM((1, 8, LANES), F32),
            pltpu.VMEM((3, 2, 8, LANES), F32),
            pltpu.VMEM((2, 2, 4, 8, PROFILE), F32),
            pltpu.VMEM((2, 2, 2, 8, PROFILE), F32),
            pltpu.VMEM((2, 2, 4, 8, PROFILE), F32),
            pltpu.VMEM((2, 2, 2, 8, PROFILE), F32),
            pltpu.VMEM((2, 7, 8, PROFILE), F32),
            block, block, block, block, block,
            pltpu.VMEM((cells, 2 * PROFILE), BF16),
            pltpu.VMEM((n_rows, cells), BF16),
            pltpu.VMEM((cells, n_rows), BF16),
            pltpu.VMEM((KINDS * PROFILE, 2 * PROFILE), BF16),
            pltpu.VMEM((KINDS * PROFILE, 2 * PROFILE), BF16),
            pltpu.VMEM((n_rows, KINDS * PROFILE), BF16),
            pltpu.VMEM((n_rows, KINDS * PROFILE), BF16),
            pltpu.VMEM((n_rows, 2 * PROFILE), BF16),
            pltpu.SemaphoreType.DMA((7,)),
            pltpu.SemaphoreType.DMA((3,)),
            pltpu.SemaphoreType.DMA((2, 2)),
            pltpu.SemaphoreType.DMA((2, 2, 2)),
            pltpu.SemaphoreType.DMA((3, 2)),
            pltpu.SemaphoreType.DMA((3, 2)),
            pltpu.SemaphoreType.DMA((2,)),
            pltpu.SemaphoreType.DMA((2,)),
            pltpu.SemaphoreType.DMA,
            pltpu.SemaphoreType.DMA((2, 2)),
            pltpu.SemaphoreType.DMA((2,)),
            pltpu.SemaphoreType.DMA((2, 6)),
            pltpu.SemaphoreType.DMA((2, 4)),
            pltpu.SemaphoreType.DMA((4,)),
            pltpu.SemaphoreType.DMA((4,)),
            pltpu.SemaphoreType.REGULAR,
        ],
        compiler_params=pltpu.CompilerParams(collective_id=0, has_side_effects=True, vmem_limit_bytes=56 * 1024 * 1024),
        name="assimilate",
    )(*(
        pltpu.with_memory_space_constraint(x, pltpu.HBM)
        for x in (
            increment.reshape(PROFILE * ROWS, LANES),
            coef_lon.reshape(FIELDS * ROWS, LANES),
            coef_lat.reshape(FIELDS * ROWS, LANES),
            obs_values,
            obs_weight,
            obs_operator,
            obs_columns.reshape(tiles, LANES),
            obs_types.reshape(tiles, LANES),
            obs_counts.reshape(1, n_lat),
        )
    ))
    return gradient.reshape(increment.shape), departures


def solution(mesh):
    return jax.shard_map(
        functools.partial(local, mesh.shape["lon"], mesh.shape["lat"]),
        mesh=mesh,
        in_specs=(
            P(None, None, "lat", "lon"),
            P(None, "lat", "lon"),
            P(None, "lat", "lon"),
            P(("lon", "lat"), None),
            P(("lon", "lat"), None),
            P(),
            P(("lon", "lat")),
            P(("lon", "lat")),
            P(("lon", "lat")),
        ),
        out_specs=(P(None, None, "lat", "lon"), P(("lon", "lat"), None)),
        check_vma=False,
    )
```

```python
import functools

import jax
import jax.numpy as jnp
from jax import lax
from jax.experimental import pallas as pl
from jax.experimental.pallas import tpu as pltpu
from jax.sharding import PartitionSpec as P

HALO = 4
STEPS = 4
ROWS = 8
EXT = ROWS + 2 * HALO
LANES = 128
SPAN = LANES // 8
WIDE = SPAN + 2 * HALO
FIELDS = 4
PROFILE = 128
KINDS = 3
F32 = jnp.float32
BF16 = jnp.bfloat16
CORNER = ((1, 0, 3), (2, 3, 2), (3, 5, 1))


def lane_iota(shape):
    return lax.broadcasted_iota(jnp.int32, shape, len(shape) - 1)


def row_iota(shape):
    return lax.broadcasted_iota(jnp.int32, shape, 0)


def split(x):
    hi = x.astype(BF16)
    return hi, (x - hi.astype(F32)).astype(BF16)


def kernel(
    n_lon, n_lat, slots,
    inc_h, clon_h, clat_h, obs_h, wgt_h, op_h, col_h, typ_h, cnt_h,
    grad_o, dep_o,
    inc_v, cf_v, op_v, col_v, typ_v, cnt_v, obs_v, wgt_v, code_v, codes_in, codet_v, dep_v,
    xa, xe, ya, za, turn_v, rows_c, tile_v, tiles_in, side_v, corner_v, from_side, from_corner, relay_v,
    root_a, root_b, mid_c, lon_c, lat_c, st_v, oh_v, oht_v, opf_v, opb_v, lhs_hi, lhs_lo, adj_v,
    load_sem, own_sem, side_send, corner_send, tile_send, row_send, recv_side, recv_corner, recv_tile, recv_row, recv_coef,
    relay_send, relay_recv, a2a_send, a2a_recv, ready_sem,
):
    lon, lat = lax.axis_index("lon"), lax.axis_index("lat")
    n_rows = n_lat * slots
    n_tiles = n_rows // LANES
    per_tile = LANES // slots
    south, north = lat == 0, lat == n_lat - 1
    south_i, north_i = south.astype(jnp.int32), north.astype(jnp.int32)
    opposite = n_lon // 2

    def lon_at(by):
        return lax.rem(lon + by + n_lon, n_lon)

    def prev_of(d):
        return (lon_at(d + opposite * south_i), lat - 1 + south_i)

    def next_of(d):
        return (lon_at(d + opposite * north_i), lat + 1 - north_i)

    last, after = lax.rem(lon, opposite) == opposite - 1, lax.rem(lon, opposite) == 0
    last_i, after_i = last.astype(jnp.int32), after.astype(jnp.int32)

    def dev(where):
        return {"lon": where[0], "lat": where[1]}

    barrier = pltpu.get_barrier_semaphore()

    def greet(where):
        pl.semaphore_signal(barrier, inc=1, device_id=dev(where), device_id_type=pl.DeviceIdType.MESH)

    for where in (prev_of(-1), next_of(-1), (lon_at(-1), lat)):
        greet(where)

    @pl.when(south)
    def _():
        greet(prev_of(0))

    @pl.when(north)
    def _():
        greet(next_of(0))

    @pl.when(last)
    def _():
        greet((lon_at(opposite), lat))

    @pl.when(after)
    def _():
        greet((lon_at(opposite), lat))
        greet((lon_at(opposite - 1), lat))

    @pl.when(after & ~south)
    def _():
        greet((lon_at(opposite - 1), lat - 1))

    @pl.when(after & ~north)
    def _():
        greet((lon_at(opposite - 1), lat + 1))

    @pl.loop(1, n_lat)
    def _(k):
        greet((lon, lax.rem(lat + k, n_lat)))

    loads = [
        pltpu.make_async_copy(src, dst, load_sem.at[i])
        for i, (src, dst) in enumerate(
            (
                (inc_h, inc_v), (clon_h, cf_v.at[0]), (clat_h, cf_v.at[1]), (op_h, op_v),
                (col_h, col_v), (typ_h, typ_v), (cnt_h, cnt_v),
            )
        )
    ]
    for load in loads:
        load.start()
    mine = pl.ds(pl.multiple_of(lat * slots, slots), slots)
    own = [
        pltpu.make_async_copy(obs_h.at[mine], obs_v.at[mine], own_sem.at[0]),
        pltpu.make_async_copy(wgt_h.at[mine], wgt_v.at[mine], own_sem.at[1]),
    ]
    for copy in own:
        copy.start()

    for i in (4, 5, 6):
        loads[i].wait()
    rep = (lane_iota((n_lat, n_rows)) // slots == row_iota((n_lat, n_rows))).astype(F32).astype(BF16)
    counts = jnp.broadcast_to(cnt_v[...].astype(F32), (8, n_lat)).astype(BF16)
    limit = jnp.dot(counts, rep, preferred_element_type=F32)
    for q in range(n_tiles):
        lim = limit[0:1, q * LANES : (q + 1) * LANES].astype(jnp.int32)
        code = col_v[q : q + 1, :] * 4 + typ_v[q : q + 1, :] + 1
        code_v[q] = jnp.where(lane_iota((1, LANES)) % slots < lim, code, 0)

    for i in (0, 1, 2):
        loads[i].wait()

    @pl.loop(0, ROWS)
    def _(r):
        turn_v[r] = jnp.transpose(inc_v[pl.ds(r, PROFILE, stride=ROWS), :])
        for i in range(SPAN):
            xa[r + HALO, HALO + i] = turn_v[r, pl.ds(i, 8, stride=SPAN), :]
        for ct in range(2):
            rows_c[r + HALO, ct * FIELDS : (ct + 1) * FIELDS, :] = cf_v[ct, pl.ds(r, FIELDS, stride=ROWS), :]

    first, end = HALO, HALO + SPAN

    def stage(phase, x):
        for r in range(ROWS):
            for j in range(HALO):
                at = r % 2 * HALO + j
                side_v[phase, 0, r // 2, at : at + 1, :] = x[r + HALO, end - HALO + j, 7:8, :]
                side_v[phase, 1, r // 2, at : at + 1, :] = x[r + HALO, first + j, 0:1, :]
        for half in range(2):
            for k, at, n in CORNER:
                r = HALO + k - 1 if half == 0 else HALO + ROWS - k
                for j in range(n):
                    corner_v[phase, half, 0, at + j : at + j + 1, :] = x[r, end - n + j, 7:8, :]
                    corner_v[phase, half, 1, at + j : at + j + 1, :] = x[r, first + j, 0:1, :]

    stage(0, xa)
    lane = lane_iota((8, LANES))
    tile = jnp.zeros((8, LANES), F32)
    for r in range(ROWS):
        v = rows_c[r + HALO]
        tile = jnp.where(lane >> 2 == r, pltpu.roll(v, 4 * r + HALO, 1), tile)
        tile = jnp.where(lane >> 2 == r + 16, pltpu.roll(v, 64 + 4 * r, 1), tile)
    tile_v[0] = tile

    pl.semaphore_wait(barrier, n_lat - 1 + 3 + south_i + north_i + last_i * (4 - south_i - north_i) + after_i)

    for by, row in ((1, lat), (1 + opposite * south_i, lat - 1 + south_i), (1 + opposite * north_i, lat + 1 - north_i)):
        by = jnp.where(last, 1 - opposite, by)
        pl.semaphore_signal(ready_sem, inc=1, device_id=dev((lon_at(by), row)), device_id_type=pl.DeviceIdType.MESH)

    low, high = pl.ds(HALO, HALO), pl.ds(2 * HALO, HALO)
    inner = pl.ds(HALO, SPAN)
    to_prev = pl.ds(3 * HALO * (1 - south_i), HALO)
    to_next = pl.ds(3 * HALO * north_i, HALO)
    prev_side, next_side = 1 - south_i, north_i

    def send(src, dst, send_at, sem, where):
        return pltpu.make_async_remote_copy(
            src_ref=src, dst_ref=dst, send_sem=send_at, recv_sem=sem,
            device_id=dev(where), device_id_type=pl.DeviceIdType.MESH,
        )

    def start(copies):
        for copy in copies:
            copy.start()
        return copies

    class Routed:
        def __init__(self, other, plain, changed):
            self.other, self.plain, self.changed = other, plain, changed

        def ahead(self):
            pl.when(self.other)(self.changed.start)

        def start(self):
            pl.when(~self.other)(self.plain.start)

        def wait_send(self):
            self.plain.wait_send()

    class Only:
        def __init__(self, holds, copy):
            self.holds, self.copy = holds, copy

        def ahead(self):
            pass

        def start(self):
            pl.when(self.holds)(self.copy.start)

        def wait_send(self):
            pl.when(self.holds)(self.copy.wait_send)

    ends = (last, after)

    def by_relay(i, part, src, send_at):
        at = relay_v.at[i, pl.ds(*((0, 4), (4, 1), (5, 1), (6, 1))[part])]
        return send(src, at, send_at, relay_recv.at[i, part], (lon_at(opposite), lat))

    def small_copies(phase, *to):
        copies = []
        for i in to:
            d = 1 - 2 * i
            src, send_at = side_v.at[phase, i], side_send.at[phase, i]
            copy = send(src, from_side.at[phase, i], send_at, recv_side.at[phase], (lon_at(d), lat))
            copies.append(copy if phase else Routed(ends[i], copy, by_relay(i, 0, src, send_at)))
            for half, side, where, pole in ((0, prev_side, prev_of(d), south), (1, next_side, next_of(d), north)):
                src, send_at = corner_v.at[phase, half, pl.ds(i, 1)], corner_send.at[phase, half, i]
                copy = send(src, from_corner.at[phase, side, pl.ds(i, 1)], send_at, recv_corner.at[phase], where)
                copies.append(copy if phase else Routed(ends[i] & ~pole, copy, by_relay(i, 1 + half, src, send_at)))
        return copies

    def tile_copies(*to):
        copies = []
        for i in to:
            d = 1 - 2 * i
            for v, (at, where, pole) in enumerate(
                ((2, (lon_at(d), lat), None), (prev_side, prev_of(d), south), (next_side, next_of(d), north))
            ):
                copy = send(tile_v, tiles_in.at[at, pl.ds(i, 1)], tile_send.at[v, i], recv_tile, where)
                if v == 0:
                    copies.append(Routed(ends[i], copy, by_relay(i, 3, tile_v, tile_send.at[v, i])))
                else:
                    copies.append(Only(~ends[i] | pole, copy))
        return copies

    def pass_on(i):
        over, end_of = lon_at((1 - opposite) * (1 - 2 * i)), ends[i]
        ways = [
            (end_of, 0, (0, 4), from_side.at[0, i], recv_side.at[0], lat),
            (end_of & ~south, 1, (4, 1), from_corner.at[0, 1, pl.ds(i, 1)], recv_corner.at[0], lat - 1),
            (end_of & ~north, 2, (5, 1), from_corner.at[0, 0, pl.ds(i, 1)], recv_corner.at[0], lat + 1),
            (end_of, 3, (6, 1), tiles_in.at[2, pl.ds(i, 1)], recv_tile, lat),
            (end_of & ~south, None, (6, 1), tiles_in.at[1, pl.ds(i, 1)], recv_tile, lat - 1),
            (end_of & ~north, None, (6, 1), tiles_in.at[0, pl.ds(i, 1)], recv_tile, lat + 1),
        ]
        copies = []
        for n, (holds, part, (at, count), dst, sem, to) in enumerate(ways):
            src = relay_v.at[i, pl.ds(at, count)]
            copy = Only(holds, send(src, dst, relay_send.at[i, n], sem, (over, to)))
            if part is not None:
                arrived = pltpu.make_async_copy(src, src, relay_recv.at[i, part])
                pl.when(holds)(arrived.wait)
            copy.start()
            copies.append(copy)
        return copies

    def row_copies(phase, x):
        return [
            send(x.at[low, inner], x.at[to_prev, inner], row_send.at[phase, 0], recv_row.at[phase, prev_side], prev_of(0)),
            send(x.at[high, inner], x.at[to_next, inner], row_send.at[phase, 1], recv_row.at[phase, next_side], next_of(0)),
        ]

    def coef_copies():
        return [
            send(rows_c.at[low], rows_c.at[to_prev], row_send.at[2, 0], recv_coef.at[prev_side], prev_of(0)),
            send(rows_c.at[high], rows_c.at[to_next], row_send.at[2, 1], recv_coef.at[next_side], next_of(0)),
        ]

    def arrive(ref, sem):
        pltpu.make_async_copy(ref, ref, sem).wait()

    eastward, westward = small_copies(0, 0) + tile_copies(0), small_copies(0, 1) + tile_copies(1)
    for copy in eastward + westward:
        copy.ahead()
    sent = start(eastward + coef_copies())

    @pl.loop(1, n_lat)
    def _(k):
        to = lax.rem(lat + k, n_lat)
        pltpu.make_async_remote_copy(
            src_ref=code_v.at[to // per_tile], dst_ref=codes_in.at[lat], send_sem=a2a_send.at[0], recv_sem=a2a_recv.at[0],
            device_id=dev((lon, to)), device_id_type=pl.DeviceIdType.MESH,
        ).start()

    sent += start(row_copies(0, xa))

    @pl.loop(1, n_lat)
    def _(k):
        to = lax.rem(lat + k, n_lat)
        theirs = pl.ds(pl.multiple_of(to * slots, slots), slots)
        for i, (src, dst) in enumerate(((obs_h, obs_v), (wgt_h, wgt_v))):
            pltpu.make_async_remote_copy(
                src_ref=src.at[theirs], dst_ref=dst.at[mine], send_sem=a2a_send.at[1 + i], recv_sem=a2a_recv.at[1 + i],
                device_id=dev((lon, to)), device_id_type=pl.DeviceIdType.MESH,
            ).start()

    def all_but_one(ref, sem):
        part = ref.at[pl.ds(0, ref.shape[0] // n_lat * (n_lat - 1))]
        pltpu.make_async_copy(part, part, sem).wait()

    loads[3].wait()
    for k in range(KINDS):
        hi, lo = split(op_v[k])
        opf_v[k * PROFILE : (k + 1) * PROFILE, :] = jnp.concatenate([hi, lo], 1)
        hi, lo = split(jnp.transpose(op_v[k]))
        opb_v[k * PROFILE : (k + 1) * PROFILE, :] = jnp.concatenate([hi, lo], 1)

    def spread_profile(table, ct):
        return jnp.transpose(
            jnp.concatenate(
                [jnp.broadcast_to(table[ct * FIELDS + f : ct * FIELDS + f + 1, :], (PROFILE // FIELDS, LANES)) for f in range(FIELDS)], 0
            )
        )

    def ghosts(x, r):
        for j in range(HALO):
            x[r, j] = pltpu.roll(x[r, end - HALO + j], 1, 0)
            x[r, end + j] = pltpu.roll(x[r, first + j], 7, 0)

    def coefficients(r):
        table = rows_c[r]
        for ct, root in enumerate((root_a, root_b)):
            turn_v[ct] = spread_profile(table, ct)
            for i in range(SPAN):
                root[r, HALO + i] = turn_v[ct, pl.ds(i, 8, stride=SPAN), :]
            ghosts(root, r)

    def products(r, places):
        for i in places:
            a, b = root_a[r, i], root_b[r, i]
            mid_c[r, i] = 1.0 - 2.0 * (a * a + b * b)
            if i < WIDE - 1:
                lon_c[r, i] = a * root_a[r, i + 1]

    def products_lat(r, places):
        for i in places:
            lat_c[r, i] = root_b[r, i] * root_b[r + 1, i]

    @pl.loop(HALO, HALO + ROWS)
    def _(r):
        coefficients(r)
        ghosts(xa, r)

    sent += pass_on(0)
    all_but_one(codes_in, a2a_recv.at[0])
    codes_in[lat] = code_v[lat // per_tile]
    mod = lax.rem(lat, per_tile)
    lane_1 = lane_iota((1, LANES))
    for q in range(n_tiles):
        row = jnp.zeros((1, LANES), jnp.int32)
        for j in range(per_tile):
            moved = pltpu.roll(codes_in[q * per_tile + j], lax.rem(LANES + slots * (j - mod), LANES), 1)
            row = jnp.where(lane_1 // slots == j, moved, row)
        cell = (row - 1) >> 2
        cell = jnp.where(row > 0, (cell & -LANES) + (cell & (SPAN - 1)) * 8 + ((cell & (LANES - 1)) >> 4), -1)
        turned = jnp.transpose(jnp.broadcast_to(row.astype(F32), (LANES, LANES))).astype(jnp.int32)
        codet_v[q * LANES : (q + 1) * LANES, :] = turned
        across = jnp.transpose(jnp.broadcast_to(cell.astype(F32), (LANES, LANES))).astype(jnp.int32)
        down = jnp.broadcast_to(cell, (LANES, LANES))
        for r in range(ROWS):
            at = r * LANES
            oh_v[q * LANES : (q + 1) * LANES, at : at + LANES] = jnp.where(across == lane_iota((LANES, LANES)) + at, 1.0, 0.0).astype(BF16)
            oht_v[at : at + LANES, q * LANES : (q + 1) * LANES] = jnp.where(down == row_iota((LANES, LANES)) + at, 1.0, 0.0).astype(BF16)

    halo_rows = (0, 1, 2, 3, 12, 13, 14, 15)
    swaps = ((0, 3), (1, 2))
    for side in range(2):
        arrive(rows_c.at[pl.ds(3 * HALO * side, HALO)], recv_coef.at[side])
    for pole, base in ((south, 0), (north, 3 * HALO)):
        @pl.when(pole)
        def _():
            for p, q in swaps:
                one, two = rows_c[base + p], rows_c[base + q]
                rows_c[base + p] = two
                rows_c[base + q] = one

    @pl.loop(0, HALO)
    def _(r):
        coefficients(r)
        coefficients(r + 3 * HALO)

    @pl.loop(0, EXT)
    def _(r):
        products(r, range(HALO, HALO + SPAN))

    @pl.loop(0, EXT - 1)
    def _(r):
        products_lat(r, range(HALO, HALO + SPAN))

    pl.semaphore_wait(ready_sem, 3)
    sent += start(westward) + pass_on(1)

    arrive(tiles_in, recv_tile)
    side_tile = jnp.zeros((8, LANES), F32)
    for i in range(2):
        in_side = (lane >> 6) == i
        for e in range(EXT):
            if e < HALO:
                table, r = tiles_in[0, i], HALO + e - (1 + 2 * e) * south_i
            elif e < HALO + ROWS:
                table, r = tiles_in[2, i], e - HALO
            else:
                j = e - HALO - ROWS
                table, r = tiles_in[1, i], j + (ROWS - 1 - 2 * j) * north_i
            if HALO <= e < HALO + ROWS and e > HALO:
                continue
            if e == HALO:
                hit = in_side & ((lane & 63) >= 4 * HALO) & ((lane & 63) < 4 * (HALO + ROWS))
                side_tile = jnp.where(hit, pltpu.roll(table, 4 * HALO, 1), side_tile)
            else:
                moved = pltpu.roll(table, lax.rem(4 * (e - r) + LANES, LANES), 1)
                side_tile = jnp.where(in_side & ((lane & 63) >> 2 == e), moved, side_tile)
    for ct, root in enumerate((root_a, root_b)):
        turn_v[2 + ct] = spread_profile(side_tile, ct)
        for e in range(EXT):
            for j in range(HALO):
                root[e, j, 0:1, :] = turn_v[2 + ct, e * HALO + j : e * HALO + j + 1, :]
                root[e, end + j, 7:8, :] = turn_v[2 + ct, 64 + e * HALO + j : 65 + e * HALO + j, :]
    edge_places = (*range(HALO), *range(end, WIDE))

    @pl.loop(0, EXT)
    def _(r):
        products(r, (*edge_places, end - 1))

    @pl.loop(0, EXT - 1)
    def _(r):
        products_lat(r, edge_places)

    sign_south = jnp.where((lane >= LANES // 2) & south, -1.0, 1.0).astype(F32)
    sign_north = jnp.where((lane >= LANES // 2) & north, -1.0, 1.0).astype(F32)

    def complete(phase, x):
        for side, (pole, sign) in enumerate(((south, sign_south), (north, sign_north))):
            base = 3 * HALO * side
            arrive(x.at[pl.ds(base, HALO), inner], recv_row.at[phase, side])

            @pl.when(pole)
            def _():
                @pl.loop(first, end)
                def _(i):
                    for p, q in swaps:
                        one, two = x[base + p, i], x[base + q, i]
                        x[base + p, i] = two * sign
                        x[base + q, i] = one * sign

        @pl.loop(0, HALO)
        def _(r):
            ghosts(x, r)
            ghosts(x, r + 3 * HALO)

        arrive(from_side.at[phase], recv_side.at[phase])
        arrive(from_corner.at[phase], recv_corner.at[phase])
        for r in range(ROWS):
            for j in range(HALO):
                at = r % 2 * HALO + j
                x[r + HALO, j, 0:1, :] = from_side[phase, 0, r // 2, at : at + 1, :]
                x[r + HALO, end + j, 7:8, :] = from_side[phase, 1, r // 2, at : at + 1, :]
        for side, sign in enumerate((sign_south, sign_north)):
            west, east = from_corner[phase, side, 0] * sign, from_corner[phase, side, 1] * sign
            for k, at, n in CORNER:
                r = HALO - k if side == 0 else HALO + ROWS - 1 + k
                for j in range(n):
                    x[r, HALO - n + j, 0:1, :] = west[at + j : at + j + 1, :]
                    x[r, end + j, 7:8, :] = east[at + j : at + j + 1, :]

    def diffuse(x):
        for t, (src, dst) in enumerate(((x, ya), (ya, za), (za, ya), (ya, za))):
            @pl.loop(t + 1, EXT - 1 - t)
            def _(r):
                f = {i: src[r, i] for i in range(t, WIDE - t)}
                for i in range(t + 1, WIDE - 1 - t):
                    dst[r, i] = (
                        mid_c[r, i] * f[i]
                        + (lon_c[r, i - 1] * f[i - 1] + lon_c[r, i] * f[i + 1])
                        + (lat_c[r - 1, i] * src[r - 1, i] + lat_c[r, i] * src[r + 1, i])
                    )

    complete(0, xa)
    diffuse(xa)

    @pl.loop(0, ROWS)
    def _(r):
        v = za[r + HALO, first:end].reshape(LANES, PROFILE)
        hi, lo = split(v)
        st_v[pl.ds(pl.multiple_of(r * LANES, LANES), LANES), :] = jnp.concatenate([hi, lo], 1)

    found = jnp.dot(oh_v[...], st_v[...], preferred_element_type=F32)
    columns = found[:, :PROFILE] + found[:, PROFILE:]

    def by_kind(values, table):
        hi, lo = split(values)
        kind = (codet_v[...] - 1) & 3
        for k in range(KINDS):
            of_kind = kind == k
            lhs_hi[:, k * PROFILE : (k + 1) * PROFILE] = jnp.where(of_kind, hi.astype(F32), 0.0).astype(BF16)
            lhs_lo[:, k * PROFILE : (k + 1) * PROFILE] = jnp.where(of_kind, lo.astype(F32), 0.0).astype(BF16)
        one = jnp.dot(lhs_hi[...], table[...], preferred_element_type=F32)
        two = jnp.dot(lhs_lo[...], table[:, :PROFILE], preferred_element_type=F32)
        return one[:, :PROFILE] + one[:, PROFILE:] + two

    model = by_kind(columns, opf_v)
    for copy in own:
        copy.wait()
    all_but_one(obs_v, a2a_recv.at[1])
    all_but_one(wgt_v, a2a_recv.at[2])
    dep = jnp.where(codet_v[...] > 0, obs_v[...] - model, 0.0)
    dep_v[...] = dep
    adj = by_kind(wgt_v[...] * dep, opb_v)
    hi, lo = split(adj)
    adj_v[...] = jnp.concatenate([hi, lo], 1)
    def send_departures(begin, stop):
        @pl.loop(begin, stop)
        def _(k):
            to = lax.rem(lat + k, n_lat)
            theirs = pl.ds(pl.multiple_of(to * slots, slots), slots)
            pltpu.make_async_remote_copy(
                src_ref=dep_v.at[theirs], dst_ref=dep_o.at[mine], send_sem=a2a_send.at[3], recv_sem=a2a_recv.at[3],
                device_id=dev((lon, to)), device_id_type=pl.DeviceIdType.MESH,
            ).start()

    early, late = n_lat * 3 // 8, n_lat * 5 // 8
    send_departures(early, late)
    forcing = jnp.dot(oht_v[...], adj_v[...], preferred_element_type=F32)
    forcing = forcing[:, :PROFILE] + forcing[:, PROFILE:]
    for r in range(ROWS):
        xe[r + HALO, first:end] = forcing[r * LANES : (r + 1) * LANES].reshape(SPAN, 8, PROFILE)
    stage(1, xe)
    sent += start(small_copies(1, 0, 1) + row_copies(1, xe))

    back = pltpu.make_async_copy(dep_v.at[mine], dep_o.at[mine], own_sem.at[2])
    back.start()

    send_departures(1, early)
    send_departures(late, n_lat)

    @pl.loop(HALO, HALO + ROWS)
    def _(r):
        ghosts(xe, r)

    complete(1, xe)
    diffuse(xe)

    @pl.loop(0, ROWS)
    def _(r):
        for i in range(SPAN):
            turn_v[r, pl.ds(i, 8, stride=SPAN), :] = za[r + HALO, HALO + i]
        rows = pl.ds(r, PROFILE, stride=ROWS)
        grad_o[rows, :] = inc_v[rows, :] - jnp.transpose(turn_v[r])

    for copy in sent:
        copy.wait_send()
    all_but_one(codes_in, a2a_send.at[0])
    all_but_one(obs_v, a2a_send.at[1])
    all_but_one(wgt_v, a2a_send.at[2])
    all_but_one(dep_v, a2a_send.at[3])
    all_but_one(dep_o, a2a_recv.at[3])
    back.wait()


def local(n_lon, n_lat, increment, coef_lon, coef_lat, obs_values, obs_weight, obs_operator, obs_columns, obs_types, obs_counts):
    n_rows = obs_columns.shape[0]
    slots = n_rows // n_lat
    tiles = n_rows // LANES
    cells = ROWS * LANES
    vmem = pl.BlockSpec(memory_space=pltpu.VMEM)
    block = pltpu.VMEM((EXT, WIDE, 8, PROFILE), F32)
    gradient, departures = pl.pallas_call(
        functools.partial(kernel, n_lon, n_lat, slots),
        out_shape=(
            jax.ShapeDtypeStruct((PROFILE * ROWS, LANES), F32),
            jax.ShapeDtypeStruct((n_rows, PROFILE), F32),
        ),
        in_specs=[pl.BlockSpec(memory_space=pltpu.HBM)] * 9,
        out_specs=(vmem, vmem),
        scratch_shapes=[
            pltpu.VMEM((PROFILE * ROWS, LANES), F32),
            pltpu.VMEM((2, FIELDS * ROWS, LANES), F32),
            pltpu.VMEM((KINDS, PROFILE, PROFILE), F32),
            pltpu.VMEM((tiles, LANES), jnp.int32),
            pltpu.VMEM((tiles, LANES), jnp.int32),
            pltpu.VMEM((1, n_lat), jnp.int32),
            pltpu.VMEM((n_rows, PROFILE), F32),
            pltpu.VMEM((n_rows, PROFILE), F32),
            pltpu.VMEM((tiles, 1, LANES), jnp.int32),
            pltpu.VMEM((n_lat, 1, LANES), jnp.int32),
            pltpu.VMEM((n_rows, LANES), jnp.int32),
            pltpu.VMEM((n_rows, PROFILE), F32),
            block, block, block, block,
            pltpu.VMEM((ROWS, LANES, PROFILE), F32),
            pltpu.VMEM((EXT, 8, LANES), F32),
            pltpu.VMEM((1, 8, LANES), F32),
            pltpu.VMEM((3, 2, 8, LANES), F32),
            pltpu.VMEM((2, 2, 4, 8, PROFILE), F32),
            pltpu.VMEM((2, 2, 2, 8, PROFILE), F32),
            pltpu.VMEM((2, 2, 4, 8, PROFILE), F32),
            pltpu.VMEM((2, 2, 2, 8, PROFILE), F32),
            pltpu.VMEM((2, 7, 8, PROFILE), F32),
            block, block, block, block, block,
            pltpu.VMEM((cells, 2 * PROFILE), BF16),
            pltpu.VMEM((n_rows, cells), BF16),
            pltpu.VMEM((cells, n_rows), BF16),
            pltpu.VMEM((KINDS * PROFILE, 2 * PROFILE), BF16),
            pltpu.VMEM((KINDS * PROFILE, 2 * PROFILE), BF16),
            pltpu.VMEM((n_rows, KINDS * PROFILE), BF16),
            pltpu.VMEM((n_rows, KINDS * PROFILE), BF16),
            pltpu.VMEM((n_rows, 2 * PROFILE), BF16),
            pltpu.SemaphoreType.DMA((7,)),
            pltpu.SemaphoreType.DMA((3,)),
            pltpu.SemaphoreType.DMA((2, 2)),
            pltpu.SemaphoreType.DMA((2, 2, 2)),
            pltpu.SemaphoreType.DMA((3, 2)),
            pltpu.SemaphoreType.DMA((3, 2)),
            pltpu.SemaphoreType.DMA((2,)),
            pltpu.SemaphoreType.DMA((2,)),
            pltpu.SemaphoreType.DMA,
            pltpu.SemaphoreType.DMA((2, 2)),
            pltpu.SemaphoreType.DMA((2,)),
            pltpu.SemaphoreType.DMA((2, 6)),
            pltpu.SemaphoreType.DMA((2, 4)),
            pltpu.SemaphoreType.DMA((4,)),
            pltpu.SemaphoreType.DMA((4,)),
            pltpu.SemaphoreType.REGULAR,
        ],
        compiler_params=pltpu.CompilerParams(collective_id=0, has_side_effects=True, vmem_limit_bytes=56 * 1024 * 1024),
        name="assimilate",
    )(*(
        pltpu.with_memory_space_constraint(x, pltpu.HBM)
        for x in (
            increment.reshape(PROFILE * ROWS, LANES),
            coef_lon.reshape(FIELDS * ROWS, LANES),
            coef_lat.reshape(FIELDS * ROWS, LANES),
            obs_values,
            obs_weight,
            obs_operator,
            obs_columns.reshape(tiles, LANES),
            obs_types.reshape(tiles, LANES),
            obs_counts.reshape(1, n_lat),
        )
    ))
    return gradient.reshape(increment.shape), departures


def solution(mesh):
    return jax.shard_map(
        functools.partial(local, mesh.shape["lon"], mesh.shape["lat"]),
        mesh=mesh,
        in_specs=(
            P(None, None, "lat", "lon"),
            P(None, "lat", "lon"),
            P(None, "lat", "lon"),
            P(("lon", "lat"), None),
            P(("lon", "lat"), None),
            P(),
            P(("lon", "lat")),
            P(("lon", "lat")),
            P(("lon", "lat")),
        ),
        out_specs=(P(None, None, "lat", "lon"), P(("lon", "lat"), None)),
        check_vma=False,
    )
```
